32 devices in a mesh: gx: 8 (over z, y), gz: 4 (over x, core).
Axes of the slice: x: 2, y: 2, z: 4, core: 2. Of those that a mesh axis runs over, the one named last changes fastest.
Arguments:
- velocity_field: float32 [3, 3072, 16, 512], P(None, 'gx', None, 'gz'), may hold values from -6 to 6
- interp_weight: bfloat16 [2048, 128, 512], P(('gx', 'gz')), may hold values from -0.25 to 0.25
- particle_velocity: float32 [3, 2048, 128], P(None, ('gx', 'gz')), may hold values from -6 to 6
- tile_owner: int32 [8192, 1], P(('gx', 'gz')), may hold values from 0 to 31; in each aligned block of 256 rows (0 to 255, 256 to 511, ...) at most 24 rows name the same one
- tile_index: int32 [8192], P(('gx', 'gz')), may hold values from 0 to 6143
- block_count: int32 [32], P(('gx', 'gz')), may hold values from 16 to 64, as said below
Outputs:
- fluid_rhs: float32 [3, 3072, 16, 512], P(None, 'gx', None, 'gz')
- new_velocity: float32 [3, 2048, 128], P(None, ('gx', 'gz'))
The draws below stay inside these ranges and needn't reach their ends.
Inputs may be any that keep to these rules, and one draw needn't show every extreme that they name: `tile_owner`: among the 256 requests of one device, no owner is named more than 24 times, a bound that some block reaches. `block_count`: some device has all 64 blocks live.
All inputs are finite; a program needn't handle non-finite values.
Results may differ from the reference program's by a relative error of at most 0.0014.
Values may be sent and summed in bfloat16 or wider, within the bound.
A program may use at most 256 MiB of HBM per device.

```python
import math
import jax
import jax.numpy as jnp
import numpy as np
from jax import lax

CX = 384
CY = 16
CZ = 128
PB = 128
BLK_DEV = 64
KT = 4
REQ_DEV = 256
CAP = 24
NX = 3072
NY = 16
NZ = 512
BLOCKS = 2048
REQS = 8192
N_GX = 8
N_GZ = 4
DEVICES = 32


def draw_block_count(key, part):
    devices = N_GX * N_GZ
    fewest = max(1, BLK_DEV // 4)
    counts = jax.random.randint(jax.random.fold_in(key, 11), (devices,), fewest, BLK_DEV + 1)
    full_at = jax.random.randint(jax.random.fold_in(key, 12), (), 0, devices)
    other_at = (full_at + 1 + jax.random.randint(jax.random.fold_in(key, 13), (), 0, devices - 1)) % devices
    counts = counts.at[full_at].set(BLK_DEV).at[other_at].set(fewest)
    return counts.astype(jnp.int32)


def touch_ends(result, rng, low, top_value):
    index_at = [jax.random.randint(jax.random.fold_in(rng, axis), (), 0, length) for axis, length in enumerate(result.shape)]
    widest = result.shape.index(max(result.shape))
    beside = index_at[:widest] + [(index_at[widest] + 1) % result.shape[widest]] + index_at[widest + 1:]
    return result.at[tuple(index_at)].set(low).at[tuple(beside)].set(top_value)


def block_levels(own_key, shape, split, low, largest):
    def one(axis_at, parts):
        heights = jax.random.uniform(jax.random.fold_in(jax.random.fold_in(own_key, 6), axis_at), (parts,), jnp.float32, low / len(split), largest / len(split))
        return jnp.repeat(jnp.exp(heights), shape[axis_at] // parts).reshape((-1,) + (1,) * (len(shape) - axis_at - 1))

    loudness = one(*split[0])
    for cut in split[1:]:
        loudness = loudness * one(*cut)
    return loudness


def deal_out(rng, own, number, rows, count, top, limit, slope):
    sequence = jax.random.permutation(rng, count)
    crowded, usual = portions_of(count, rows * top, limit, slope, True), portions_of(count, rows * top, limit, slope, False)
    places = jnp.arange(count)

    def named(lengths, turn):
        used = int((lengths > 0).sum())
        fixed = max(1, used // 4)
        passed = fixed + (places - fixed + turn * (used - fixed)) % max(1, count - fixed)
        return jnp.zeros((count,), jnp.int32).at[sequence[jnp.where(places < fixed, places, passed)]].set(jnp.asarray(lengths, jnp.int32))

    lengths = jnp.where(number % 4 == 0, named(crowded, number // 4), named(usual, number - number // 4 - 1))
    mixed = jax.random.permutation(jax.random.fold_in(own, 3), count)
    giver, receiver = mixed[0:count // 2 * 2:2], mixed[1:count // 2 * 2:2]
    slack = jnp.minimum(lengths[giver] - 1, limit - lengths[receiver]) // 2
    slack = jnp.where((giver == sequence[0]) | (receiver == sequence[0]) | (lengths[receiver] == 0), 0, jnp.maximum(slack, 0))
    passed = jax.random.randint(jax.random.fold_in(own, 4), (count // 2,), 0, 1 << 20) % (slack + 1)
    lengths = lengths.at[giver].add(-passed).at[receiver].add(passed)
    labels = jnp.searchsorted(jnp.cumsum(lengths), jnp.arange(rows * top), side="right").astype(jnp.int32)
    table = labels.reshape(top, rows).T
    table = table[jax.random.permutation(jax.random.fold_in(own, 1), rows)]
    turn = jax.random.randint(jax.random.fold_in(own, 2), (rows, 1), 0, top)
    return jnp.take_along_axis(table, (jnp.arange(top)[None, :] + turn) % top, axis=1)


def portions_of(number_of, total, limit, skew, full):
    weights = [(1 << 20) // math.isqrt(standing ** skew) + 1 for standing in range(1, number_of + 1)]
    largest = limit if full else min(limit, max(-(-total // number_of), total * weights[0] // sum(weights)))
    least = 1 if total - largest >= number_of - 1 else 0
    given, surplus = [largest] + [least] * (number_of - 1), total - largest - least * (number_of - 1)
    while surplus > 0:
        free = [i for i in range(1, number_of) if given[i] < largest] or [i for i in range(1, number_of) if given[i] < limit]
        pool, left = sum([weights[i] for i in free]), surplus
        for i in free:
            addition = min(limit - given[i], max(1, left * weights[i] // pool), surplus)
            given[i] = given[i] + addition
            surplus = surplus - addition
    return np.array(given)


def bell_draw(rng, dims, spread, bound, cuts=(), kind=jnp.bfloat16):
    array = spread * jax.random.normal(rng, dims, jnp.float32)
    if cuts:
        array = array * block_levels(rng, dims, cuts, -0.22, 0.18)
    return jnp.clip(array, -bound, bound).astype(kind)


def setup_inputs(seed: int = 0) -> dict:
    streams_of = jax.random.split(jax.random.key(seed), 7)
    velocity_field = bell_draw(streams_of[0], (3, NX, NY, NZ), 1.0, 6.0, ((1, 8), (3, 4)), jnp.float32)
    interp_weight = bell_draw(streams_of[1], (BLOCKS, PB, KT * CZ), (KT * CZ) ** -0.5, 0.25, ((0, 32),))
    particle_velocity = bell_draw(streams_of[2], (3, BLOCKS, PB), 1.0, 6.0, ((1, 32),), jnp.float32)
    tile_owner_keys = jax.random.split(jax.random.fold_in(streams_of[3], 1), REQS // REQ_DEV)
    tile_owner_turns = jax.random.permutation(jax.random.fold_in(streams_of[3], 3), REQS // REQ_DEV)
    tile_owner = jax.vmap(lambda own, number: deal_out(jax.random.fold_in(streams_of[3], 2), own, number, REQ_DEV, DEVICES, 1, CAP, 2))(tile_owner_keys, tile_owner_turns).reshape((REQS, 1))
    tile_index = touch_ends(jax.random.randint(streams_of[4], (REQS,), 0, CX * CY), jax.random.fold_in(streams_of[4], 1), 0, (CX * CY) - 1).astype(jnp.int32)
    block_count = draw_block_count(jax.random.fold_in(streams_of[6], 71), 0)
    return dict(velocity_field=velocity_field, interp_weight=interp_weight, particle_velocity=particle_velocity, tile_owner=tile_owner, tile_index=tile_index, block_count=block_count)


ALPHA = 1.0 / 3.0
A_COEF = 14.0 / 9.0
B_COEF = 1.0 / 9.0
VISCOSITY = 0.2
RELAX_TIME = 1.0
TIME_STEP = 0.5
LOADING = 0.5


def derivative(field):
    length = field.shape[0]
    wavenum = jnp.arange(length // 2 + 1).astype(field.dtype) * (2.0 * math.pi / length)
    symbol = (A_COEF * jnp.sin(wavenum) + 0.5 * B_COEF * jnp.sin(2.0 * wavenum)) / (1.0 + 2.0 * ALPHA * jnp.cos(wavenum))
    spectrum = jnp.fft.rfft(field, axis=0)
    return jnp.fft.irfft(spectrum * (1j * symbol)[:, None, None], n=length, axis=0).astype(field.dtype)


def particle_step(items):
    weights, tile_data, velocity, live_mask = items
    wide = weights.astype(jnp.float32)
    sampled = jnp.einsum("bpm,cbm->cbp", wide, tile_data.astype(jnp.float32), precision=lax.Precision.HIGHEST)
    drag_accel = live_mask[None, :, None] * (sampled - velocity) / RELAX_TIME
    new_velocity = velocity + TIME_STEP * drag_accel
    drag_half = lax.optimization_barrier(drag_accel.astype(jnp.bfloat16))
    push_back = -LOADING * jnp.einsum("bpm,cbp->cbm", wide, drag_half.astype(jnp.float32), precision=lax.Precision.HIGHEST)
    return new_velocity, push_back


def reference(velocity_field, interp_weight, particle_velocity, tile_owner, tile_index, block_count):
    devices = N_GX * N_GZ
    stream_comp = velocity_field[0]
    pieces = []
    for axis_comp in range(3):
        component = velocity_field[axis_comp]
        advect = 0.5 * (derivative(stream_comp * component) + stream_comp * derivative(component))
        span_curve = jnp.roll(component, -1, 2) - 2.0 * component + jnp.roll(component, 1, 2)
        pieces.append(-advect + VISCOSITY * span_curve)
    fluid = jnp.stack(pieces)
    owners = tile_owner[:, 0]
    slab_row = (owners // N_GZ) * CX + tile_index // CY
    wall_row = tile_index % CY
    span_piece = owners % N_GZ
    blocked = velocity_field.reshape(3, NX, NY, N_GZ, CZ)
    tile_data = blocked[:, slab_row, wall_row, span_piece, :].astype(jnp.bfloat16)
    tile_data = tile_data.reshape(3, devices, BLK_DEV, KT * CZ).transpose(1, 0, 2, 3)
    weights = interp_weight.reshape(devices, BLK_DEV, PB, KT * CZ)
    velocity = particle_velocity.reshape(3, devices, BLK_DEV, PB).transpose(1, 0, 2, 3)
    live_mask = (jnp.arange(BLK_DEV, dtype=jnp.int32)[None, :] < block_count[:, None]).astype(velocity_field.dtype)
    moved, push_back = lax.map(particle_step, (weights, tile_data, velocity, live_mask))
    new_velocity = moved.transpose(1, 0, 2, 3).reshape(3, devices * BLK_DEV, PB)
    push_back = push_back.transpose(1, 0, 2, 3).reshape(3, devices * BLK_DEV * KT, CZ)
    feedback = jnp.zeros((3, NX, NY, N_GZ, CZ), velocity_field.dtype).at[:, slab_row, wall_row, span_piece, :].add(push_back)
    fluid_rhs = fluid + feedback.reshape(3, NX, NY, NZ)
    return fluid_rhs, new_velocity
```

```python
import functools
import math

import jax
import jax.numpy as jnp
from jax import lax
from jax.experimental import pallas as pl
from jax.experimental.pallas import tpu as pltpu
from jax.sharding import PartitionSpec as P

ROOT = (math.sqrt(5.0) / 3.0 - 1.0) * 1.5
GREEN_GAIN = 3.0 / math.sqrt(5.0)
GAMMA = (25.0 / 36.0) * GREEN_GAIN * (1.0 - ROOT * ROOT)
EPS = (1.0 / 12.0) / GAMMA
VISCOSITY = 0.2
RELAX_TIME = 1.0
TIME_STEP = 0.5
LOADING = 0.5
WINDOW = 48
F32 = jnp.float32
BF16 = jnp.bfloat16
VMEM_LIMIT = 40 * 1024 * 1024


def iota(shape, dim):
    return lax.broadcasted_iota(jnp.int32, shape, dim)


def dot(a, b, ca, cb):
    return lax.dot_general(a, b, (((ca,), (cb,)), ((), ())), preferred_element_type=F32)


def end_lanes(span):
    corner = (8, span)
    first = (iota(corner, 0) == 0) & (iota(corner, 1) == 0)
    second = (iota(corner, 0) == 1) & (iota(corner, 1) == span - 1)
    return jnp.where(first | second, 1.0, 0.0)


def request_slots(kt, pitch, devices, me, owner_row, index_row):
    count = owner_row.shape[1]
    blocks = count // kt
    r = iota((count, 1), 0)
    cols = iota((count, count), 1)
    pick = cols == kt * (r % blocks) + r // blocks
    owner = jnp.sum(jnp.where(pick, owner_row, 0), 1, keepdims=True)
    index = jnp.sum(jnp.where(pick, index_row, 0), 1, keepdims=True)
    onehot = (owner == iota((count, devices), 1)).astype(F32)
    lower = (cols <= r).astype(F32).astype(BF16)
    turned = onehot.astype(BF16)
    seen = dot(lower, turned, 1, 0)
    position = jnp.sum(seen * onehot, 1, keepdims=True).astype(jnp.int32) - 1
    place = (position + me * pitch) % 128 == iota((count, 128), 1)
    high = jnp.where(place, (index // 128).astype(F32), 0.0).astype(BF16)
    low = jnp.where(place, (index % 128).astype(F32), 0.0).astype(BF16)
    high_sum, low_sum = dot(turned, high, 0, 0), dot(turned, low, 0, 0)
    send = high_sum.astype(jnp.int32) * 128 + low_sum.astype(jnp.int32)
    return owner * pitch + position, send


def advance(fields, carry):
    state, before = carry[:6], carry[6:]
    parts = [EPS * f + s for f, s in zip(before, state)]
    sums = [parts[3 + c] + fields[0] * parts[c] for c in range(3)]
    moved = [f + ROOT * s for f, s in zip(fields, state)]
    return sums, tuple(moved) + tuple(fields)


def step_kernel(
    sizes, owner_ref, index_ref, live_ref, velocity_ref, field_hbm, weight_hbm,
    fluid_ref, back_ref, got_ref, moved_ref,
    field_ref, weight_ref, table_ref, send_ref, got_smem, slot_ref, slot_row_ref, rows_ref, tile_ref, reply_ref,
    staged_ref, own_ref, push_ref, outgoing_ref,
    my_low, my_high, my_left, my_right, low_ref, high_ref, left_ref, right_ref, halo_ref,
    field_sem, weight_sem, smem_sem, send_sem, recv_sem, tile_send, tile_recv, back_send, back_recv, edge_send, edge_recv,
):
    gx, gz, kt, window = sizes
    devices = gx * gz
    wall, span = my_left.shape[1:]
    lines = field_ref.shape[1]
    slab = lines // wall
    pitch = tile_ref.shape[1]
    slots = devices * pitch
    x, z = lax.axis_index("gx"), lax.axis_index("gz")
    me = x * gz + z
    fetch = pltpu.make_async_copy(field_hbm, field_ref, field_sem)
    fetch.start()
    fetch_weight = pltpu.make_async_copy(weight_hbm, weight_ref, weight_sem)

    barrier = pltpu.get_barrier_semaphore()

    def partner(n):
        j = n // gz
        dx = lax.rem(gx // 2 + (1 - 2 * (j % 2)) * ((j + 1) // 2) + gx, gx)
        return lax.rem(x + dx, gx), lax.rem(z + lax.rem(n + 1, gz), gz)

    def source(n):
        j = n // gz
        dx = lax.rem(gx // 2 + (1 - 2 * (j % 2)) * ((j + 1) // 2) + gx, gx)
        return lax.rem(x + gx - dx, gx) * gz + lax.rem(z + gz - lax.rem(n + 1, gz), gz)

    def each(body):
        def one(n, carry):
            body(n)
            return carry

        lax.fori_loop(0, devices - 1, one, 0)

    def greet(n):
        pl.semaphore_signal(barrier, inc=1, device_id=partner(n), device_id_type=pl.DeviceIdType.MESH)

    each(greet)
    slot, send = request_slots(kt, pitch, devices, me, owner_ref[...], index_ref[...])
    slot_ref[...] = slot
    table_ref[...] = send
    for d in range(devices):
        send_ref[d] = table_ref[d : d + 1, :]
    pl.semaphore_wait(barrier, devices - 1)

    def exchange(src, dst, sent, got):
        def at(n):
            peer = partner(n)
            return pltpu.make_async_remote_copy(
                src_ref=src.at[peer[0] * gz + peer[1]],
                dst_ref=dst.at[me],
                send_sem=sent.at[n],
                recv_sem=got.at[n],
                device_id=peer,
                device_id_type=pl.DeviceIdType.MESH,
            )

        return at

    parcel = exchange(send_ref, got_ref, send_sem, recv_sem)
    tiles = exchange(tile_ref, reply_ref, tile_send, tile_recv)
    pushes = exchange(outgoing_ref, back_ref, back_send, back_recv)

    each(lambda n: parcel(n).start())
    got_ref[me] = send_ref[me]
    fetch.wait()
    fetch_weight.start()

    def edge(k, src, dst, peer):
        return pltpu.make_async_remote_copy(
            src_ref=src,
            dst_ref=dst,
            send_sem=edge_send.at[k],
            recv_sem=edge_recv.at[k],
            device_id=peer,
            device_id_type=pl.DeviceIdType.MESH,
        )

    edges = [
        edge(0, my_right, left_ref, (lax.rem(x + 1, gx), z)),
        edge(1, my_left, right_ref, (lax.rem(x + gx - 1, gx), z)),
        edge(2, my_high, low_ref, (x, lax.rem(z + 1, gz))),
        edge(3, my_low, high_ref, (x, lax.rem(z + gz - 1, gz))),
    ]

    def line(i):
        return pl.ds(pl.multiple_of(i * wall, wall), wall)

    def load(i):
        u = [field_ref[c, line(i), :] for c in range(3)]
        return u + [u[0] * u[c] for c in range(3)]

    zero = jnp.zeros((wall, span), F32)

    def moments(order):
        def one(i, state):
            return tuple(f + ROOT * s for f, s in zip(load(order(i)), state))

        return lax.fori_loop(0, window, one, (zero,) * 6, unroll=4)

    for k, value in enumerate(moments(lambda i: slab - window + i)):
        my_right[k] = value
    for c in range(3):
        my_right[6 + c] = field_ref[c, lines - wall :, :]
    edges[0].start()
    for k, value in enumerate(moments(lambda i: window - 1 - i)):
        my_left[k] = value
    for c in range(3):
        my_left[6 + c] = field_ref[c, :wall, :]
    edges[1].start()

    def up(i, carry):
        sums, carry = advance(load(i), carry)
        for c in range(3):
            fluid_ref[c, line(i), :] = 0.5 * GAMMA * sums[c]
        return carry

    lax.fori_loop(0, slab, up, (zero,) * 12, unroll=4)

    each(lambda n: parcel(n).wait())
    copy = pltpu.make_async_copy(got_ref, got_smem, smem_sem)
    copy.start()
    copy.wait()

    def collect(peer):
        for k in range(pitch):
            row = jnp.minimum(jnp.maximum(got_smem[peer, 0, (peer * pitch + k) % 128], 0), lines - 1)
            for c in range(3):
                rows_ref[c, k : k + 1, :] = field_ref[c, pl.ds(row, 1), :]
        for c in range(3):
            tile_ref[peer, :, c * span : (c + 1) * span] = rows_ref[c].astype(BF16)

    def gather(n):
        peer = partner(n)
        collect(peer[0] * gz + peer[1])
        tiles(n).start()

    each(gather)
    collect(me)
    reply_ref[me] = tile_ref[me]

    def down(n, carry):
        i = slab - 1 - n
        sums, carry = advance(load(i), carry)
        for c in range(3):
            fluid_ref[c, line(i), :] = fluid_ref[c, line(i), :] - 0.5 * GAMMA * sums[c]
        return carry

    lax.fori_loop(0, slab, down, (zero,) * 12, unroll=4)

    span_rows = window
    pick = end_lanes(span).astype(BF16)
    for c in range(3):
        for n in range(slab // span_rows):
            part = slice(n * span_rows * wall, (n + 1) * span_rows * wall)
            lanes = dot(pick, field_ref[c, part].astype(BF16), 1, 1)
            my_low[c, :, part] = lanes[0:1]
            my_high[c, :, part] = lanes[1:2]
    edges[2].start()
    edges[3].start()

    count = slot_ref.shape[0]
    same = iota((count, count), 0) == iota((count, count), 1)
    slot_row_ref[...] = jnp.sum(jnp.where(same, slot_ref[...], 0), 0, keepdims=True)

    def border(ref):
        u = [ref[6 + c] for c in range(3)]
        return [ref[k] for k in range(6)], u + [u[0] * u[c] for c in range(3)]

    def spread(ref, gain, order):
        state, before = border(ref)

        def add(i, parts):
            u0 = field_ref[0, line(i), :]
            for c in range(3):
                fluid_ref[c, line(i), :] = fluid_ref[c, line(i), :] + gain * (parts[3 + c] + u0 * parts[c])

        add(order(0), [EPS * f + s for f, s in zip(before, state)])

        def one(n, state):
            add(order(n), state)
            return tuple(ROOT * s for s in state)

        lax.fori_loop(1, window, one, tuple(ROOT * s for s in state), unroll=2)

    edges[0].wait()
    spread(left_ref, 0.5 * GAMMA, lambda n: n)
    edges[1].wait()
    spread(right_ref, -0.5 * GAMMA, lambda n: slab - 1 - n)

    def stage(at):
        staged_ref[pl.ds(pl.multiple_of(at * pitch, pitch), pitch), :] = reply_ref[at].astype(F32)

    stage(me)

    def receive(n):
        tiles(n).wait()
        stage(source(n))

    each(receive)

    particles, cells = weight_ref.shape[1:]
    blocks = count // kt
    chosen = jnp.where(slot_ref[...] == iota((count, slots), 1), 1.0, 0.0).astype(BF16)
    own = dot(chosen, staged_ref[...].astype(BF16), 1, 0)
    for j in range(kt):
        for c in range(3):
            own_ref[c, :, j * span : (j + 1) * span] = own[j * blocks : (j + 1) * blocks, c * span : (c + 1) * span]
    fetch_weight.wait()
    group = 16 if blocks % 16 == 0 else 8
    live_blocks = live_ref[0]

    def particle(step, carry):
        base = pl.multiple_of(step * group, group)
        tile = jnp.concatenate([own_ref[c, pl.ds(base, group), :] for c in range(3)], 0).astype(BF16)
        row = iota((3 * group, particles), 0) % group
        sampled = jnp.zeros((3 * group, particles), F32)
        for b in range(0, group, 2):
            both = dot(tile, weight_ref[pl.ds(base + b, 2)].reshape(2 * particles, cells), 1, 1)
            sampled = jnp.where(row == b, both[:, :particles], sampled)
            sampled = jnp.where(row == b + 1, both[:, particles:], sampled)
        velocity = jnp.concatenate([velocity_ref[c, pl.ds(base, group), :] for c in range(3)], 0)
        live = jnp.where(row + base < live_blocks, 1.0, 0.0)
        drag = live * (sampled - velocity) * (1.0 / RELAX_TIME)
        moved = velocity + TIME_STEP * drag
        for c in range(3):
            moved_ref[c, pl.ds(base, group), :] = moved[c * group : (c + 1) * group]
        half = drag.astype(BF16)
        row = iota((3 * group, cells), 0) % group
        push = jnp.zeros((3 * group, cells), F32)
        for b in range(group):
            push = jnp.where(row == b, dot(half, weight_ref[base + b], 1, 0), push)
        push = -LOADING * push
        for j in range(kt):
            for c in range(3):
                push_ref[pl.ds(j * blocks + base, group), c * span : (c + 1) * span] = push[
                    c * group : (c + 1) * group, j * span : (j + 1) * span
                ]
        return carry

    lax.fori_loop(0, blocks // group, particle, 0)

    lot = 8
    pushed = push_ref[...].astype(BF16)
    for q in range(devices // lot):
        named = jnp.where(iota((lot * pitch, count), 0) + q * lot * pitch == slot_row_ref[...], 1.0, 0.0).astype(BF16)
        placed = dot(named, pushed, 1, 0)
        for p in range(lot):
            outgoing_ref[q * lot + p] = placed[p * pitch : (p + 1) * pitch].astype(BF16)
    each(lambda n: pushes(n).start())
    back_ref[me] = outgoing_ref[me]

    edges[2].wait()
    edges[3].wait()
    lane = iota((wall, span), 1)
    rows = halo_ref.shape[1] // wall
    shape = (8, rows * wall)
    first, second = iota(shape, 0) == 0, iota(shape, 0) == 1

    def chunk(n, carry):
        at = pl.ds(pl.multiple_of(n * rows * wall, rows * wall), rows * wall)
        for c in range(3):
            ends = jnp.where(first, low_ref[c, :, at], jnp.where(second, high_ref[c, :, at], 0.0))
            halo_ref[c] = dot(ends.astype(BF16), pick, 0, 0)

        def one(i, carry):
            here = line(n * rows + i)
            for c in range(3):
                u = field_ref[c, here, :]
                near = jnp.where(lane == 0, 0.0, pltpu.roll(u, 1, 1))
                far = jnp.where(lane == span - 1, 0.0, pltpu.roll(u, span - 1, 1))
                curve = near + far + halo_ref[c, line(i), :] - 2.0 * u
                fluid_ref[c, here, :] = fluid_ref[c, here, :] + VISCOSITY * curve
            return carry

        return lax.fori_loop(0, rows, one, carry, unroll=4)

    lax.fori_loop(0, slab // rows, chunk, 0)
    each(lambda n: pushes(n).wait())


def add_kernel(got_ref, fluid_ref, back_ref, moved_ref, out_hbm, moved_out, named_ref, total_ref, out_ref, out_sem):
    devices, pitch, width = back_ref.shape
    lines, span = fluid_ref.shape[1:]
    slots = devices * pitch
    moved_out[...] = moved_ref[...]
    given = got_ref[...].reshape(devices, 128)
    for g in range(slots // 128):
        flat = iota((devices, 128), 1) + g * 128 - pitch * iota((devices, 128), 0)
        named_ref[:, g * 128 : (g + 1) * 128] = jnp.sum(
            jnp.where((flat >= 0) & (flat < pitch), given, 0), 0, keepdims=True
        )
    for p in range(devices):
        total_ref[p * pitch : (p + 1) * pitch, :] = back_ref[p].astype(F32)
    returned = total_ref[...].astype(BF16)
    size = 256

    def leave(n):
        at = pl.ds(pl.multiple_of(n * size, size), size)
        return pltpu.make_async_copy(out_ref.at[:, at, :], out_hbm.at[:, at, :], out_sem.at[n])

    def one(n, carry):
        local = named_ref[...] - n * size
        local = jnp.where((local >= 0) & (local < size), local, -1).astype(F32).astype(BF16)
        ids = iota((size, slots), 0).astype(F32).astype(BF16)
        named = jnp.where(ids == local, jnp.ones((), BF16), jnp.zeros((), BF16))
        total = dot(named, returned, 1, 0)
        at = pl.ds(pl.multiple_of(n * size, size), size)
        for c in range(3):
            out_ref[c, at, :] = fluid_ref[c, at, :] + total[:, c * span : (c + 1) * span]
        leave(n).start()
        return carry

    lax.fori_loop(0, lines // size, one, 0)

    def finish(n, carry):
        leave(n).wait()
        return carry

    lax.fori_loop(0, lines // size, finish, 0)


def vmem():
    return pl.BlockSpec(memory_space=pltpu.VMEM)


def smem():
    return pl.BlockSpec(memory_space=pltpu.SMEM)


def hbm():
    return pl.BlockSpec(memory_space=pltpu.HBM)


def params():
    return pltpu.CompilerParams(vmem_limit_bytes=VMEM_LIMIT)


def cost(flops, nbytes):
    return pl.CostEstimate(flops=int(flops), bytes_accessed=int(nbytes), transcendentals=0)


def shards(velocity_field, interp_weight, particle_velocity, tile_owner, tile_index, block_count):
    _, slab, wall, span = velocity_field.shape
    shape = jax.ShapeDtypeStruct
    gx, gz = lax.axis_size("gx"), lax.axis_size("gz")
    devices = gx * gz
    requests = tile_index.shape[0]
    blocks, particles, cells = interp_weight.shape
    kt = requests // blocks
    pitch = -(-max(2, 3 * requests // devices) // 8) * 8
    slots = devices * pitch
    field_bytes = velocity_field.size * 4

    window = WINDOW if slab % WINDOW == 0 else slab
    lines = slab * wall
    dma = pltpu.SemaphoreType.DMA
    fluid, back, got, moved = pl.pallas_call(
        functools.partial(step_kernel, (gx, gz, kt, window)),
        out_shape=(
            pltpu.VMEM((3, lines, span), F32),
            pltpu.VMEM((devices, pitch, 3 * span), BF16),
            pltpu.VMEM((devices, 1, 128), jnp.int32),
            pltpu.VMEM(particle_velocity.shape, F32),
        ),
        in_specs=[vmem(), vmem(), smem(), vmem(), hbm(), hbm()],
        out_specs=(vmem(),) * 4,
        scratch_shapes=[
            pltpu.VMEM((3, lines, span), F32),
            pltpu.VMEM(interp_weight.shape, BF16),
            pltpu.VMEM((devices, 128), jnp.int32),
            pltpu.VMEM((devices, 1, 128), jnp.int32),
            pltpu.SMEM((devices, 1, 128), jnp.int32),
            pltpu.VMEM((requests, 1), jnp.int32),
            pltpu.VMEM((1, requests), jnp.int32),
            pltpu.VMEM((3, pitch, span), F32),
            pltpu.VMEM((devices, pitch, 3 * span), BF16),
            pltpu.VMEM((devices, pitch, 3 * span), BF16),
            pltpu.VMEM((slots, 3 * span), F32),
            pltpu.VMEM((3, blocks, cells), F32),
            pltpu.VMEM((requests, 3 * span), F32),
            pltpu.VMEM((devices, pitch, 3 * span), BF16),
            pltpu.VMEM((3, 1, lines), F32),
            pltpu.VMEM((3, 1, lines), F32),
            pltpu.VMEM((9, wall, span), F32),
            pltpu.VMEM((9, wall, span), F32),
            pltpu.VMEM((3, 1, lines), F32),
            pltpu.VMEM((3, 1, lines), F32),
            pltpu.VMEM((9, wall, span), F32),
            pltpu.VMEM((9, wall, span), F32),
            pltpu.VMEM((3, window * wall, span), F32),
            dma,
            dma,
            dma,
            dma((devices,)),
            dma((devices,)),
            dma((devices,)),
            dma((devices,)),
            dma((devices,)),
            dma((devices,)),
            dma((4,)),
            dma((4,)),
        ],
        compiler_params=pltpu.CompilerParams(
            vmem_limit_bytes=VMEM_LIMIT, collective_id=0, has_side_effects=True
        ),
        cost_estimate=cost(5e8, field_bytes + interp_weight.size * 2),
        name="step",
    )(
        tile_owner.reshape(1, requests),
        tile_index.reshape(1, requests),
        block_count,
        particle_velocity,
        velocity_field.reshape(3, lines, span),
        interp_weight,
    )

    result, moved = pl.pallas_call(
        add_kernel,
        out_shape=(shape((3, lines, span), F32), shape(particle_velocity.shape, F32)),
        in_specs=[vmem()] * 4,
        out_specs=(hbm(), vmem()),
        scratch_shapes=[
            pltpu.VMEM((1, slots), jnp.int32),
            pltpu.VMEM((slots, 3 * span), F32),
            pltpu.VMEM((3, lines, span), F32),
            dma((lines // 256,)),
        ],
        compiler_params=params(),
        cost_estimate=cost(2.0 * lines * slots * 3 * span, field_bytes * 2),
        name="feedback",
    )(got, fluid, back, moved)
    return (result.reshape(velocity_field.shape), moved)


def solution(mesh):
    placed = (
        P(None, "gx", None, "gz"),
        P(("gx", "gz"), None, None),
        P(None, ("gx", "gz"), None),
        P(("gx", "gz"), None),
        P(("gx", "gz")),
        P(("gx", "gz")),
    )
    return jax.shard_map(
        shards,
        mesh=mesh,
        in_specs=placed,
        out_specs=(P(None, "gx", None, "gz"), P(None, ("gx", "gz"), None)),
        check_vma=False,
    )
```

```python
import functools
import math

import jax
import jax.numpy as jnp
from jax import lax
from jax.experimental import pallas as pl
from jax.experimental.pallas import tpu as pltpu
from jax.sharding import PartitionSpec as P

ROOT = (math.sqrt(5.0) / 3.0 - 1.0) * 1.5
GREEN_GAIN = 3.0 / math.sqrt(5.0)
GAMMA = (25.0 / 36.0) * GREEN_GAIN * (1.0 - ROOT * ROOT)
EPS = (1.0 / 12.0) / GAMMA
VISCOSITY = 0.2
RELAX_TIME = 1.0
TIME_STEP = 0.5
LOADING = 0.5
WINDOW = 48
EARLY = 4
CURVE = 1536
SPREAD = 1024
PIECES = 6
F32 = jnp.float32
BF16 = jnp.bfloat16
VMEM_LIMIT = 40 * 1024 * 1024


def iota(shape, dim):
    return lax.broadcasted_iota(jnp.int32, shape, dim)


def dot(a, b, ca, cb):
    return lax.dot_general(a, b, (((ca,), (cb,)), ((), ())), preferred_element_type=F32)


def end_lanes(span):
    corner = (8, span)
    first = (iota(corner, 0) == 0) & (iota(corner, 1) == 0)
    second = (iota(corner, 0) == 1) & (iota(corner, 1) == span - 1)
    return jnp.where(first | second, 1.0, 0.0)


def halo_lanes(span):
    shape = (8, 3 * span)
    row, lane = iota(shape, 0), iota(shape, 1)
    first = (row == lane // span) & (lane % span == 0)
    last = (row == lane // span + 3) & (lane % span == span - 1)
    return jnp.where(first | last, 1.0, 0.0).astype(BF16)


def second_difference(span):
    shape = (2 * span, span)
    row, lane = iota(shape, 0) % span, iota(shape, 1)
    beside = (row == lane + 1) | (row + 1 == lane)
    return jnp.where(row == lane, -2.0, jnp.where(beside, 1.0, 0.0)).astype(BF16)


def request_slots(kt, pitch, gx, gz, x, z, owner_row, index_row):
    count, devices = owner_row.shape[1], gx * gz
    blocks = count // kt
    r = iota((count, 1), 0)
    cols = iota((count, count), 1)
    pick = cols == kt * (r % blocks) + r // blocks
    owner = jnp.sum(jnp.where(pick, owner_row, 0), 1, keepdims=True)
    index = jnp.sum(jnp.where(pick, index_row, 0), 1, keepdims=True)
    away = (owner // gz + (gx - x)) % gx - gx // 2
    turn = jnp.where(away > 0, 2 * away, jnp.where(away < 0, -2 * away - 1, 0))
    order = (gx - 1 - turn) * gz + (owner % gz + (2 * gz - z - 1)) % gz
    onehot = (order == iota((count, devices), 1)).astype(F32)
    lower = (cols <= r).astype(F32).astype(BF16)
    turned = onehot.astype(BF16)
    seen = dot(lower, turned, 1, 0)
    position = jnp.sum(seen * onehot, 1, keepdims=True).astype(jnp.int32) - 1
    slot = order * pitch + position
    place = slot % 128 == iota((count, 128), 1)
    high = jnp.where(place, (index // 128).astype(F32), 0.0).astype(BF16)
    low = jnp.where(place, (index % 128).astype(F32), 0.0).astype(BF16)
    high_sum, low_sum = dot(turned, high, 0, 0), dot(turned, low, 0, 0)
    send = high_sum.astype(jnp.int32) * 128 + low_sum.astype(jnp.int32)
    return slot, send


def advance(fields, carry):
    state, before = carry[:6], carry[6:]
    parts = [EPS * f + s for f, s in zip(before, state)]
    sums = [parts[3 + c] + fields[0] * parts[c] for c in range(3)]
    moved = [f + ROOT * s for f, s in zip(fields, state)]
    return sums, tuple(moved) + tuple(fields)


def step_kernel(
    sizes, owner_hbm, index_hbm, live_ref, velocity_hbm, field_hbm, weight_hbm,
    fluid_ref, late_ref, late_index_ref, moved_ref,
    owner_ref, index_ref, velocity_ref, back_ref, got_ref, names_ref, field_ref, weight_ref, table_ref, send_ref, got_smem, slot_ref, slot_row_ref, rows_ref, tile_ref, reply_ref,
    staged_ref, own_ref, push_ref, outgoing_ref,
    my_low, my_high, my_left, my_right, low_ref, high_ref, left_ref, right_ref,
    input_sem, field_sem, weight_sem, smem_sem, send_sem, recv_sem, tile_send, tile_recv, back_send, back_recv, edge_send, edge_recv,
):
    gx, gz, kt, window = sizes
    devices = gx * gz
    wall, span = my_left.shape[1:]
    lines = field_ref.shape[1]
    slab = lines // wall
    pitch = tile_ref.shape[1]
    slots = devices * pitch
    x, z = lax.axis_index("gx"), lax.axis_index("gz")
    inputs = [
        pltpu.make_async_copy(src, dst, input_sem.at[k])
        for k, (src, dst) in enumerate(((owner_hbm, owner_ref), (index_hbm, index_ref), (velocity_hbm, velocity_ref)))
    ]
    inputs[0].start()
    inputs[1].start()
    fetch = pltpu.make_async_copy(field_hbm, field_ref, field_sem)
    fetch_weight = pltpu.make_async_copy(weight_hbm, weight_ref, weight_sem)

    barrier = pltpu.get_barrier_semaphore()

    def peer(p, way):
        j = gx - 1 - p // gz
        dx = gx // 2 + (1 - 2 * (j % 2)) * ((j + 1) // 2)
        dz = p % gz + 1
        return lax.rem(x + way * dx + 2 * gx, gx), lax.rem(z + way * dz + 2 * gz, gz)

    mine = gz - 1

    def each(body):
        def one(u, carry):
            t = u // gz
            t = (1 - t % 2) * (t // 2) + t % 2 * (gx - 1 - t // 2)
            body(t * gz + u % gz)
            return carry

        lax.fori_loop(0, mine, one, 0)
        lax.fori_loop(mine + 1, devices, one, 0)

    def greet(p):
        pl.semaphore_signal(barrier, inc=1, device_id=peer(p, 1), device_id_type=pl.DeviceIdType.MESH)

    each(greet)
    fetch.start()
    inputs[0].wait()
    inputs[1].wait()
    slot, send = request_slots(kt, pitch, gx, gz, x, z, owner_ref[...], index_ref[...])
    slot_ref[...] = slot
    table_ref[...] = send
    for d in range(devices):
        send_ref[d] = table_ref[d : d + 1, :]
    pl.semaphore_wait(barrier, devices - 1)

    def exchange(src, dst, sent, got, way):
        def at(p):
            return pltpu.make_async_remote_copy(
                src_ref=src.at[p],
                dst_ref=dst.at[p],
                send_sem=sent.at[p],
                recv_sem=got.at[p],
                device_id=peer(p, way),
                device_id_type=pl.DeviceIdType.MESH,
            )

        return at

    parcel = exchange(send_ref, got_ref, send_sem, recv_sem, 1)
    tiles = exchange(tile_ref, reply_ref, tile_send, tile_recv, -1)
    pushes = exchange(outgoing_ref, back_ref, back_send, back_recv, 1)

    each(lambda n: parcel(n).start())
    got_ref[mine] = send_ref[mine]
    fetch.wait()
    fetch_weight.start()
    inputs[2].start()

    def edge(k, src, dst, peer):
        return pltpu.make_async_remote_copy(
            src_ref=src,
            dst_ref=dst,
            send_sem=edge_send.at[k],
            recv_sem=edge_recv.at[k],
            device_id=peer,
            device_id_type=pl.DeviceIdType.MESH,
        )

    edges = [
        edge(0, my_right, left_ref, (lax.rem(x + 1, gx), z)),
        edge(1, my_left, right_ref, (lax.rem(x + gx - 1, gx), z)),
        edge(2, my_high, low_ref, (x, lax.rem(z + 1, gz))),
        edge(3, my_low, high_ref, (x, lax.rem(z + gz - 1, gz))),
    ]

    def line(i):
        return pl.ds(pl.multiple_of(i * wall, wall), wall)

    def load(i):
        u = [field_ref[c, line(i), :] for c in range(3)]
        return u + [u[0] * u[c] for c in range(3)]

    zero = jnp.zeros((wall, span), F32)

    def moments(order):
        def one(i, state):
            return tuple(f + ROOT * s for f, s in zip(load(order(i)), state))

        return lax.fori_loop(0, window, one, (zero,) * 6, unroll=4)

    for k, value in enumerate(moments(lambda i: slab - window + i)):
        my_right[k] = value
    for c in range(3):
        my_right[6 + c] = field_ref[c, lines - wall :, :]
    edges[0].start()
    for k, value in enumerate(moments(lambda i: window - 1 - i)):
        my_left[k] = value
    for c in range(3):
        my_left[6 + c] = field_ref[c, :wall, :]
    edges[1].start()

    def up(i, carry):
        sums, carry = advance(load(i), carry)
        for c in range(3):
            fluid_ref[c, line(i), :] = 0.5 * GAMMA * sums[c]
        return carry

    ends = end_lanes(span).astype(BF16)
    span_rows = window
    for c in range(3):
        for n in range(slab // span_rows):
            part = slice(n * span_rows * wall, (n + 1) * span_rows * wall)
            lanes = dot(ends, field_ref[c, part].astype(BF16), 1, 1)
            my_low[c, :, part] = lanes[0:1]
            my_high[c, :, part] = lanes[1:2]
    edges[2].start()
    edges[3].start()
    early = slab * EARLY // 8
    carry = lax.fori_loop(0, early, up, (zero,) * 12, unroll=4)

    each(lambda n: parcel(n).wait())
    copy = pltpu.make_async_copy(got_ref, got_smem, smem_sem)
    copy.start()
    copy.wait()

    def collect(p):
        for k in range(pitch):
            row = jnp.minimum(jnp.maximum(got_smem[p, 0, lax.rem(p * pitch + k, 128)], 0), lines - 1)
            for c in range(3):
                rows_ref[c, k : k + 1, :] = field_ref[c, pl.ds(row, 1), :]
        for c in range(3):
            tile_ref[p, :, c * span : (c + 1) * span] = rows_ref[c].astype(BF16)

    def gather(p):
        collect(p)
        tiles(p).start()

    each(gather)
    collect(mine)
    reply_ref[mine] = tile_ref[mine]

    lax.fori_loop(early, slab, up, carry, unroll=4)

    edges[2].wait()
    edges[3].wait()
    long = CURVE if lines % CURVE == 0 else lines
    pick, curl = halo_lanes(span), second_difference(span)

    def curve(n, carry):
        at = pl.ds(pl.multiple_of(n * long, long), long)
        row = iota((8, long), 0)
        halo = jnp.zeros((8, long), F32)
        for c in range(3):
            halo = jnp.where(row == c, low_ref[c, :, at], jnp.where(row == c + 3, high_ref[c, :, at], halo))
        halo = dot(halo.astype(BF16), pick, 0, 0)
        for c in range(3):
            u = field_ref[c, at, :]
            head = u.astype(BF16)
            rest = (u - head.astype(F32)).astype(BF16)
            inside = dot(jnp.concatenate([head, rest], 1), curl, 1, 0)
            total = inside + halo[:, c * span : (c + 1) * span]
            fluid_ref[c, at, :] = fluid_ref[c, at, :] + VISCOSITY * total
        return carry

    lax.fori_loop(0, lines // long, curve, 0)

    count = slot_ref.shape[0]
    same = iota((count, count), 0) == iota((count, count), 1)
    slot_row_ref[...] = jnp.sum(jnp.where(same, slot_ref[...], 0), 0, keepdims=True)

    def stage(src, p):
        staged_ref[pl.ds(pl.multiple_of(p * pitch, pitch), pitch), :] = src[p].astype(F32)

    stage(reply_ref, mine)

    def receive(p):
        tiles(p).wait()
        stage(reply_ref, p)

    each(receive)

    particles, cells = weight_ref.shape[1:]
    blocks = count // kt
    chosen = jnp.where(slot_ref[...] == iota((count, slots), 1), 1.0, 0.0).astype(BF16)
    own = dot(chosen, staged_ref[...].astype(BF16), 1, 0)
    for j in range(kt):
        for c in range(3):
            own_ref[c, :, j * span : (j + 1) * span] = own[j * blocks : (j + 1) * blocks, c * span : (c + 1) * span]
    fetch_weight.wait()
    inputs[2].wait()
    group = 16 if blocks % 16 == 0 else 8
    live_blocks = live_ref[0]

    def particle(step, carry):
        base = pl.multiple_of(step * group, group)
        tile = jnp.concatenate([own_ref[c, pl.ds(base, group), :] for c in range(3)], 0).astype(BF16)
        row = iota((3 * group, particles), 0) % group
        sampled = jnp.zeros((3 * group, particles), F32)
        for b in range(0, group, 2):
            both = dot(tile, weight_ref[pl.ds(base + b, 2)].reshape(2 * particles, cells), 1, 1)
            sampled = jnp.where(row == b, both[:, :particles], sampled)
            sampled = jnp.where(row == b + 1, both[:, particles:], sampled)
        velocity = jnp.concatenate([velocity_ref[c, pl.ds(base, group), :] for c in range(3)], 0)
        live = jnp.where(row + base < live_blocks, 1.0, 0.0)
        drag = live * (sampled - velocity) * (1.0 / RELAX_TIME)
        moved = velocity + TIME_STEP * drag
        for c in range(3):
            moved_ref[c, pl.ds(base, group), :] = moved[c * group : (c + 1) * group]
        half = drag.astype(BF16)
        row = iota((3 * group, cells), 0) % group
        push = jnp.zeros((3 * group, cells), F32)
        for b in range(group):
            push = jnp.where(row == b, dot(half, weight_ref[base + b], 1, 0), push)
        push = -LOADING * push
        for j in range(kt):
            for c in range(3):
                push_ref[pl.ds(j * blocks + base, group), c * span : (c + 1) * span] = push[
                    c * group : (c + 1) * group, j * span : (j + 1) * span
                ]
        return carry

    lax.fori_loop(0, blocks // group, particle, 0)

    pushed = push_ref[...].astype(BF16)
    lot = 8
    for q in range(devices // lot):
        named = jnp.where(iota((lot * pitch, count), 0) + q * lot * pitch == slot_row_ref[...], 1.0, 0.0).astype(BF16)
        placed = dot(named, pushed, 1, 0)
        for p in range(lot):
            outgoing_ref[q * lot + p] = placed[p * pitch : (p + 1) * pitch].astype(BF16)
    each(lambda p: pushes(p).start())
    back_ref[mine] = outgoing_ref[mine]

    def down(n, carry):
        i = slab - 1 - n
        sums, carry = advance(load(i), carry)
        for c in range(3):
            fluid_ref[c, line(i), :] = fluid_ref[c, line(i), :] - 0.5 * GAMMA * sums[c]
        return carry

    lax.fori_loop(0, slab, down, (zero,) * 12, unroll=4)

    def border(ref):
        u = [ref[6 + c] for c in range(3)]
        return [ref[k] for k in range(6)], u + [u[0] * u[c] for c in range(3)]

    def spread(ref, gain, order):
        state, before = border(ref)

        def add(i, parts):
            u0 = field_ref[0, line(i), :]
            for c in range(3):
                fluid_ref[c, line(i), :] = fluid_ref[c, line(i), :] + gain * (parts[3 + c] + u0 * parts[c])

        add(order(0), [EPS * f + s for f, s in zip(before, state)])

        def one(n, state):
            add(order(n), state)
            return tuple(ROOT * s for s in state)

        lax.fori_loop(1, window, one, tuple(ROOT * s for s in state), unroll=2)

    edges[0].wait()
    spread(left_ref, 0.5 * GAMMA, lambda n: n)
    edges[1].wait()
    spread(right_ref, -0.5 * GAMMA, lambda n: slab - 1 - n)

    for g in range(slots // 128):
        row = jnp.zeros((1, 128), jnp.int32)
        for p in range(g * 128 // pitch, min(devices, (g * 128 + 127) // pitch + 1)):
            flat = iota((1, 128), 1) + (g * 128 - p * pitch)
            row = jnp.where((flat >= 0) & (flat < pitch), got_ref[p], row)
        names_ref[:, g * 128 : (g + 1) * 128] = row

    def take(p, carry):
        pushes(p).wait()
        stage(back_ref, p)
        return carry

    soon = slots - late_ref.shape[0]
    first = -(-soon // pitch)
    stage(back_ref, mine)
    lax.fori_loop(0, mine, take, 0)
    lax.fori_loop(mine + 1, first, take, 0)
    size = SPREAD if lines % SPREAD == 0 else lines
    batch = staged_ref[:soon, :].astype(BF16)

    def returned(n, carry):
        at = pl.ds(pl.multiple_of(n * size, size), size)
        named = jnp.where(iota((size, soon), 0) + n * size == names_ref[:, :soon], 1.0, 0.0).astype(BF16)
        total = dot(named, batch, 1, 0)
        for c in range(3):
            fluid_ref[c, at, :] = fluid_ref[c, at, :] + total[:, c * span : (c + 1) * span]
        return carry

    lax.fori_loop(0, lines // size, returned, 0)
    lax.fori_loop(first, devices, take, 0)
    late_ref[...] = staged_ref[soon:, :].astype(BF16)
    late_index_ref[...] = names_ref[:, soon:]


def add_kernel(fluid_ref, late_ref, late_index_ref, moved_ref, out_hbm, moved_out, out_ref, out_sem):
    lines, span = fluid_ref.shape[1:]
    size = lines // out_sem.shape[0]
    width = late_ref.shape[0]

    def leave(n):
        at = pl.ds(pl.multiple_of(n * size, size), size)
        return pltpu.make_async_copy(out_ref.at[:, at, :], out_hbm.at[:, at, :], out_sem.at[n])

    def one(n, carry):
        named = jnp.where(iota((size, width), 0) + n * size == late_index_ref[...], 1.0, 0.0).astype(BF16)
        total = dot(named, late_ref[...], 1, 0)
        at = pl.ds(pl.multiple_of(n * size, size), size)
        for c in range(3):
            out_ref[c, at, :] = fluid_ref[c, at, :] + total[:, c * span : (c + 1) * span]
        leave(n).start()
        return carry

    lax.fori_loop(0, lines // size, one, 0)
    moved_out[...] = moved_ref[...]

    def finish(n, carry):
        leave(n).wait()
        return carry

    lax.fori_loop(0, lines // size, finish, 0)


def vmem():
    return pl.BlockSpec(memory_space=pltpu.VMEM)


def smem():
    return pl.BlockSpec(memory_space=pltpu.SMEM)


def hbm():
    return pl.BlockSpec(memory_space=pltpu.HBM)


def params():
    return pltpu.CompilerParams(vmem_limit_bytes=VMEM_LIMIT)


def cost(flops, nbytes):
    return pl.CostEstimate(flops=int(flops), bytes_accessed=int(nbytes), transcendentals=0)


def in_hbm(array):
    return pltpu.with_memory_space_constraint(array, pltpu.HBM)


def shards(velocity_field, interp_weight, particle_velocity, tile_owner, tile_index, block_count):
    _, slab, wall, span = velocity_field.shape
    shape = jax.ShapeDtypeStruct
    gx, gz = lax.axis_size("gx"), lax.axis_size("gz")
    devices = gx * gz
    requests = tile_index.shape[0]
    blocks, particles, cells = interp_weight.shape
    kt = requests // blocks
    pitch = -(-max(2, 3 * requests // devices) // 8) * 8
    slots = devices * pitch
    field_bytes = velocity_field.size * 4

    window = WINDOW if slab % WINDOW == 0 else slab
    lines = slab * wall
    dma = pltpu.SemaphoreType.DMA
    width = slots - 256
    fluid, late, late_index, moved = pl.pallas_call(
        functools.partial(step_kernel, (gx, gz, kt, window)),
        out_shape=(
            pltpu.VMEM((3, lines, span), F32),
            pltpu.VMEM((width, 3 * span), BF16),
            pltpu.VMEM((1, width), jnp.int32),
            pltpu.VMEM(particle_velocity.shape, F32),
        ),
        in_specs=[hbm(), hbm(), smem(), hbm(), hbm(), hbm()],
        out_specs=(vmem(),) * 4,
        scratch_shapes=[
            pltpu.VMEM((1, requests), jnp.int32),
            pltpu.VMEM((1, requests), jnp.int32),
            pltpu.VMEM(particle_velocity.shape, F32),
            pltpu.VMEM((devices, pitch, 3 * span), BF16),
            pltpu.VMEM((devices, 1, 128), jnp.int32),
            pltpu.VMEM((1, slots), jnp.int32),
            pltpu.VMEM((3, lines, span), F32),
            pltpu.VMEM(interp_weight.shape, BF16),
            pltpu.VMEM((devices, 128), jnp.int32),
            pltpu.VMEM((devices, 1, 128), jnp.int32),
            pltpu.SMEM((devices, 1, 128), jnp.int32),
            pltpu.VMEM((requests, 1), jnp.int32),
            pltpu.VMEM((1, requests), jnp.int32),
            pltpu.VMEM((3, pitch, span), F32),
            pltpu.VMEM((devices, pitch, 3 * span), BF16),
            pltpu.VMEM((devices, pitch, 3 * span), BF16),
            pltpu.VMEM((slots, 3 * span), F32),
            pltpu.VMEM((3, blocks, cells), F32),
            pltpu.VMEM((requests, 3 * span), F32),
            pltpu.VMEM((devices, pitch, 3 * span), BF16),
            pltpu.VMEM((3, 1, lines), F32),
            pltpu.VMEM((3, 1, lines), F32),
            pltpu.VMEM((9, wall, span), F32),
            pltpu.VMEM((9, wall, span), F32),
            pltpu.VMEM((3, 1, lines), F32),
            pltpu.VMEM((3, 1, lines), F32),
            pltpu.VMEM((9, wall, span), F32),
            pltpu.VMEM((9, wall, span), F32),
            dma((3,)),
            dma,
            dma,
            dma,
            dma((devices,)),
            dma((devices,)),
            dma((devices,)),
            dma((devices,)),
            dma((devices,)),
            dma((devices,)),
            dma((4,)),
            dma((4,)),
        ],
        compiler_params=pltpu.CompilerParams(
            vmem_limit_bytes=VMEM_LIMIT, collective_id=0, has_side_effects=True
        ),
        cost_estimate=cost(5e8, field_bytes + interp_weight.size * 2),
        name="step",
    )(
        in_hbm(tile_owner.reshape(1, requests)),
        in_hbm(tile_index.reshape(1, requests)),
        block_count,
        in_hbm(particle_velocity),
        in_hbm(velocity_field.reshape(3, lines, span)),
        in_hbm(interp_weight),
    )

    result, moved = pl.pallas_call(
        add_kernel,
        out_shape=(shape((3, lines, span), F32), shape(particle_velocity.shape, F32)),
        in_specs=[vmem()] * 4,
        out_specs=(hbm(), vmem()),
        scratch_shapes=[pltpu.VMEM((3, lines, span), F32), dma((PIECES if lines % (8 * PIECES) == 0 else 1,))],
        compiler_params=params(),
        cost_estimate=cost(2.0 * lines * width * 3 * span, field_bytes * 2),
        name="feedback",
    )(fluid, late, late_index, moved)
    return (result.reshape(velocity_field.shape), moved)


def solution(mesh):
    placed = (
        P(None, "gx", None, "gz"),
        P(("gx", "gz"), None, None),
        P(None, ("gx", "gz"), None),
        P(("gx", "gz"), None),
        P(("gx", "gz")),
        P(("gx", "gz")),
    )
    return jax.shard_map(
        shards,
        mesh=mesh,
        in_specs=placed,
        out_specs=(P(None, "gx", None, "gz"), P(None, ("gx", "gz"), None)),
        check_vma=False,
    )
```

```python
import functools
import math

import jax
import jax.numpy as jnp
from jax import lax
from jax.experimental import pallas as pl
from jax.experimental.pallas import tpu as pltpu
from jax.sharding import PartitionSpec as P

ROOT = (math.sqrt(5.0) / 3.0 - 1.0) * 1.5
GREEN_GAIN = 3.0 / math.sqrt(5.0)
GAMMA = (25.0 / 36.0) * GREEN_GAIN * (1.0 - ROOT * ROOT)
EPS = (1.0 / 12.0) / GAMMA
VISCOSITY = 0.2
RELAX_TIME = 1.0
TIME_STEP = 0.5
LOADING = 0.5
WINDOW = 48
EARLY = 1
CURVE = 1536
CURVE_EARLY = 1
SPREAD = 1024
PIECES = 6
F32 = jnp.float32
BF16 = jnp.bfloat16
VMEM_LIMIT = 40 * 1024 * 1024


def iota(shape, dim):
    return lax.broadcasted_iota(jnp.int32, shape, dim)


def dot(a, b, ca, cb):
    return lax.dot_general(a, b, (((ca,), (cb,)), ((), ())), preferred_element_type=F32)


def end_lanes(span):
    corner = (8, span)
    first = (iota(corner, 0) == 0) & (iota(corner, 1) == 0)
    second = (iota(corner, 0) == 1) & (iota(corner, 1) == span - 1)
    return jnp.where(first | second, 1.0, 0.0)


def halo_lanes(span):
    shape = (8, 3 * span)
    row, lane = iota(shape, 0), iota(shape, 1)
    first = (row == lane // span) & (lane % span == 0)
    last = (row == lane // span + 3) & (lane % span == span - 1)
    return jnp.where(first | last, 1.0, 0.0).astype(BF16)


def second_difference(span):
    shape = (2 * span, span)
    row, lane = iota(shape, 0) % span, iota(shape, 1)
    beside = (row == lane + 1) | (row + 1 == lane)
    return jnp.where(row == lane, -2.0, jnp.where(beside, 1.0, 0.0)).astype(BF16)


def request_slots(kt, pitch, gx, gz, x, z, owner_row, index_row):
    count, devices = owner_row.shape[1], gx * gz
    blocks = count // kt
    r = iota((count, 1), 0)
    cols = iota((count, count), 1)
    pick = cols == kt * (r % blocks) + r // blocks
    owner = jnp.sum(jnp.where(pick, owner_row, 0), 1, keepdims=True)
    index = jnp.sum(jnp.where(pick, index_row, 0), 1, keepdims=True)
    away = (owner // gz + (gx - x)) % gx - gx // 2
    turn = jnp.where(away > 0, 2 * away, jnp.where(away < 0, -2 * away - 1, 0))
    order = (gx - 1 - turn) * gz + (owner % gz + (2 * gz - z - 1)) % gz
    onehot = (order == iota((count, devices), 1)).astype(F32)
    lower = (cols <= r).astype(F32).astype(BF16)
    turned = onehot.astype(BF16)
    seen = dot(lower, turned, 1, 0)
    position = jnp.sum(seen * onehot, 1, keepdims=True).astype(jnp.int32) - 1
    slot = order * pitch + position
    place = slot % 128 == iota((count, 128), 1)
    high = jnp.where(place, (index // 128).astype(F32), 0.0).astype(BF16)
    low = jnp.where(place, (index % 128).astype(F32), 0.0).astype(BF16)
    high_sum, low_sum = dot(turned, high, 0, 0), dot(turned, low, 0, 0)
    send = high_sum.astype(jnp.int32) * 128 + low_sum.astype(jnp.int32)
    return slot, send


def advance(fields, carry):
    state, before = carry[:6], carry[6:]
    parts = [EPS * f + s for f, s in zip(before, state)]
    sums = [parts[3 + c] + fields[0] * parts[c] for c in range(3)]
    moved = [f + ROOT * s for f, s in zip(fields, state)]
    return sums, tuple(moved) + tuple(fields)


def step_kernel(
    sizes, owner_hbm, index_hbm, live_ref, velocity_hbm, field_hbm, weight_hbm,
    fluid_ref, late_ref, late_index_ref, moved_ref,
    owner_ref, index_ref, velocity_ref, back_ref, got_ref, names_ref, field_ref, weight_ref, turned_ref, table_ref, send_ref, got_smem, slot_ref, slot_row_ref, rows_ref, tile_ref, reply_ref,
    staged_ref, own_ref, push_ref, outgoing_ref,
    my_low, my_high, my_left, my_right, low_ref, high_ref, left_ref, right_ref,
    input_sem, field_sem, weight_sem, smem_sem, send_sem, recv_sem, tile_send, tile_recv, back_send, back_recv, edge_send, edge_recv,
):
    gx, gz, kt, window = sizes
    devices = gx * gz
    wall, span = my_left.shape[1:]
    lines = field_ref.shape[1]
    slab = lines // wall
    pitch = tile_ref.shape[1]
    slots = devices * pitch
    x, z = lax.axis_index("gx"), lax.axis_index("gz")
    inputs = [
        pltpu.make_async_copy(src, dst, input_sem.at[k])
        for k, (src, dst) in enumerate(((owner_hbm, owner_ref), (index_hbm, index_ref), (velocity_hbm, velocity_ref)))
    ]
    inputs[0].start()
    inputs[1].start()
    fetch = pltpu.make_async_copy(field_hbm, field_ref, field_sem)
    fetch_weight = pltpu.make_async_copy(weight_hbm, weight_ref, weight_sem)

    barrier = pltpu.get_barrier_semaphore()

    def peer(p, way):
        j = gx - 1 - p // gz
        dx = gx // 2 + (1 - 2 * (j % 2)) * ((j + 1) // 2)
        dz = p % gz + 1
        return lax.rem(x + way * dx + 2 * gx, gx), lax.rem(z + way * dz + 2 * gz, gz)

    mine = gz - 1

    def each(body):
        def one(u, carry):
            t = u // gz
            t = (1 - t % 2) * (t // 2) + t % 2 * (gx - 1 - t // 2)
            body(t * gz + u % gz)
            return carry

        lax.fori_loop(0, mine, one, 0)
        lax.fori_loop(mine + 1, devices, one, 0)

    def greet(p):
        pl.semaphore_signal(barrier, inc=1, device_id=peer(p, 1), device_id_type=pl.DeviceIdType.MESH)

    each(greet)
    fetch.start()
    inputs[0].wait()
    inputs[1].wait()
    slot, send = request_slots(kt, pitch, gx, gz, x, z, owner_ref[...], index_ref[...])
    slot_ref[...] = slot
    table_ref[...] = send
    for d in range(devices):
        send_ref[d] = table_ref[d : d + 1, :]
    pl.semaphore_wait(barrier, devices - 1)

    def exchange(src, dst, sent, got, way):
        def at(p):
            return pltpu.make_async_remote_copy(
                src_ref=src.at[p],
                dst_ref=dst.at[p],
                send_sem=sent.at[p],
                recv_sem=got.at[p],
                device_id=peer(p, way),
                device_id_type=pl.DeviceIdType.MESH,
            )

        return at

    parcel = exchange(send_ref, got_ref, send_sem, recv_sem, 1)
    tiles = exchange(tile_ref, reply_ref, tile_send, tile_recv, -1)
    pushes = exchange(outgoing_ref, back_ref, back_send, back_recv, 1)

    each(lambda n: parcel(n).start())
    got_ref[mine] = send_ref[mine]
    fetch.wait()
    fetch_weight.start()
    inputs[2].start()

    def edge(k, src, dst, peer):
        return pltpu.make_async_remote_copy(
            src_ref=src,
            dst_ref=dst,
            send_sem=edge_send.at[k],
            recv_sem=edge_recv.at[k],
            device_id=peer,
            device_id_type=pl.DeviceIdType.MESH,
        )

    edges = [
        edge(0, my_right, left_ref, (lax.rem(x + 1, gx), z)),
        edge(1, my_left, right_ref, (lax.rem(x + gx - 1, gx), z)),
        edge(2, my_high, low_ref, (x, lax.rem(z + 1, gz))),
        edge(3, my_low, high_ref, (x, lax.rem(z + gz - 1, gz))),
    ]

    def line(i):
        return pl.ds(pl.multiple_of(i * wall, wall), wall)

    def load(i):
        u = [field_ref[c, line(i), :] for c in range(3)]
        return u + [u[0] * u[c] for c in range(3)]

    zero = jnp.zeros((wall, span), F32)

    def moments(order):
        def one(i, state):
            return tuple(f + ROOT * s for f, s in zip(load(order(i)), state))

        return lax.fori_loop(0, window, one, (zero,) * 6, unroll=4)

    for k, value in enumerate(moments(lambda i: slab - window + i)):
        my_right[k] = value
    for c in range(3):
        my_right[6 + c] = field_ref[c, lines - wall :, :]
    edges[0].start()
    for k, value in enumerate(moments(lambda i: window - 1 - i)):
        my_left[k] = value
    for c in range(3):
        my_left[6 + c] = field_ref[c, :wall, :]
    edges[1].start()

    def up(i, carry):
        sums, carry = advance(load(i), carry)
        for c in range(3):
            fluid_ref[c, line(i), :] = 0.5 * GAMMA * sums[c]
        return carry

    ends = end_lanes(span).astype(BF16)
    span_rows = window
    for c in range(3):
        for n in range(slab // span_rows):
            part = slice(n * span_rows * wall, (n + 1) * span_rows * wall)
            lanes = dot(ends, field_ref[c, part].astype(BF16), 1, 1)
            my_low[c, :, part] = lanes[0:1]
            my_high[c, :, part] = lanes[1:2]
    edges[2].start()
    edges[3].start()
    early = slab * EARLY // 8
    carry = lax.fori_loop(0, early, up, (zero,) * 12, unroll=4)

    each(lambda n: parcel(n).wait())
    copy = pltpu.make_async_copy(got_ref, got_smem, smem_sem)
    copy.start()
    copy.wait()

    def collect(p):
        for k in range(pitch):
            row = jnp.minimum(jnp.maximum(got_smem[p, 0, lax.rem(p * pitch + k, 128)], 0), lines - 1)
            for c in range(3):
                rows_ref[c, k : k + 1, :] = field_ref[c, pl.ds(row, 1), :]
        for c in range(3):
            tile_ref[p, :, c * span : (c + 1) * span] = rows_ref[c].astype(BF16)

    def gather(p):
        collect(p)
        tiles(p).start()

    each(gather)
    collect(mine)
    reply_ref[mine] = tile_ref[mine]

    lax.fori_loop(early, slab, up, carry, unroll=4)

    particles, cells = weight_ref.shape[1:]
    fetch_weight.wait()

    def turn(n, carry):
        for b in range(2):
            turned_ref[n, :, b * particles : (b + 1) * particles] = jnp.transpose(weight_ref[2 * n + b])
        return carry

    lax.fori_loop(0, turned_ref.shape[0], turn, 0)
    edges[2].wait()
    edges[3].wait()
    long = CURVE if lines % CURVE == 0 else lines
    pick, curl = halo_lanes(span), second_difference(span)

    def curve(n, carry):
        at = pl.ds(pl.multiple_of(n * long, long), long)
        row = iota((8, long), 0)
        halo = jnp.zeros((8, long), F32)
        for c in range(3):
            halo = jnp.where(row == c, low_ref[c, :, at], jnp.where(row == c + 3, high_ref[c, :, at], halo))
        halo = dot(halo.astype(BF16), pick, 0, 0)
        for c in range(3):
            u = field_ref[c, at, :]
            head = u.astype(BF16)
            rest = (u - head.astype(F32)).astype(BF16)
            inside = dot(jnp.concatenate([head, rest], 1), curl, 1, 0)
            total = inside + halo[:, c * span : (c + 1) * span]
            fluid_ref[c, at, :] = fluid_ref[c, at, :] + VISCOSITY * total
        return carry

    half_way = lines // long * CURVE_EARLY // 4
    lax.fori_loop(0, half_way, curve, 0)

    count = slot_ref.shape[0]
    same = iota((count, count), 0) == iota((count, count), 1)
    slot_row_ref[...] = jnp.sum(jnp.where(same, slot_ref[...], 0), 0, keepdims=True)

    def stage(src, p):
        staged_ref[pl.ds(pl.multiple_of(p * pitch, pitch), pitch), :] = src[p].astype(F32)

    stage(reply_ref, mine)

    def receive(p):
        tiles(p).wait()
        stage(reply_ref, p)

    each(receive)

    blocks = count // kt
    chosen = jnp.where(slot_ref[...] == iota((count, slots), 1), 1.0, 0.0).astype(BF16)
    own = dot(chosen, staged_ref[...].astype(BF16), 1, 0)
    for j in range(kt):
        for c in range(3):
            own_ref[c, :, j * span : (j + 1) * span] = own[j * blocks : (j + 1) * blocks, c * span : (c + 1) * span]
    inputs[2].wait()
    group = 16 if blocks % 16 == 0 else 8
    live_blocks = live_ref[0]

    def particle(step, carry):
        base = pl.multiple_of(step * group, group)
        tile = jnp.concatenate([own_ref[c, pl.ds(base, group), :] for c in range(3)], 0).astype(BF16)
        row = iota((3 * group, particles), 0) % group
        sampled = jnp.zeros((3 * group, particles), F32)
        for b in range(0, group, 2):
            both = dot(tile, turned_ref[base // 2 + b // 2], 1, 0)
            sampled = jnp.where(row == b, both[:, :particles], sampled)
            sampled = jnp.where(row == b + 1, both[:, particles:], sampled)
        velocity = jnp.concatenate([velocity_ref[c, pl.ds(base, group), :] for c in range(3)], 0)
        live = jnp.where(row + base < live_blocks, 1.0, 0.0)
        drag = live * (sampled - velocity) * (1.0 / RELAX_TIME)
        moved = velocity + TIME_STEP * drag
        for c in range(3):
            moved_ref[c, pl.ds(base, group), :] = moved[c * group : (c + 1) * group]
        half = drag.astype(BF16)
        row = iota((3 * group, cells), 0) % group
        push = jnp.zeros((3 * group, cells), F32)
        for b in range(group):
            push = jnp.where(row == b, dot(half, weight_ref[base + b], 1, 0), push)
        push = -LOADING * push
        for j in range(kt):
            for c in range(3):
                push_ref[pl.ds(j * blocks + base, group), c * span : (c + 1) * span] = push[
                    c * group : (c + 1) * group, j * span : (j + 1) * span
                ]
        return carry

    lax.fori_loop(0, blocks // group, particle, 0, unroll=True)

    pushed = push_ref[...].astype(BF16)
    lot = 8
    for q in range(devices // lot):
        named = jnp.where(iota((lot * pitch, count), 0) + q * lot * pitch == slot_row_ref[...], 1.0, 0.0).astype(BF16)
        placed = dot(named, pushed, 1, 0)
        for p in range(lot):
            outgoing_ref[q * lot + p] = placed[p * pitch : (p + 1) * pitch].astype(BF16)
    each(lambda p: pushes(p).start())
    back_ref[mine] = outgoing_ref[mine]

    def down(n, carry):
        i = slab - 1 - n
        sums, carry = advance(load(i), carry)
        for c in range(3):
            fluid_ref[c, line(i), :] = fluid_ref[c, line(i), :] - 0.5 * GAMMA * sums[c]
        return carry

    lax.fori_loop(0, slab, down, (zero,) * 12, unroll=4)

    def border(ref):
        u = [ref[6 + c] for c in range(3)]
        return [ref[k] for k in range(6)], u + [u[0] * u[c] for c in range(3)]

    def spread(ref, gain, order):
        state, before = border(ref)

        def add(i, parts):
            u0 = field_ref[0, line(i), :]
            for c in range(3):
                fluid_ref[c, line(i), :] = fluid_ref[c, line(i), :] + gain * (parts[3 + c] + u0 * parts[c])

        add(order(0), [EPS * f + s for f, s in zip(before, state)])

        def one(n, state):
            add(order(n), state)
            return tuple(ROOT * s for s in state)

        lax.fori_loop(1, window, one, tuple(ROOT * s for s in state), unroll=2)

    edges[0].wait()
    spread(left_ref, 0.5 * GAMMA, lambda n: n)
    edges[1].wait()
    spread(right_ref, -0.5 * GAMMA, lambda n: slab - 1 - n)

    lax.fori_loop(half_way, lines // long, curve, 0)
    for g in range(slots // 128):
        row = jnp.zeros((1, 128), jnp.int32)
        for p in range(g * 128 // pitch, min(devices, (g * 128 + 127) // pitch + 1)):
            flat = iota((1, 128), 1) + (g * 128 - p * pitch)
            row = jnp.where((flat >= 0) & (flat < pitch), got_ref[p], row)
        names_ref[:, g * 128 : (g + 1) * 128] = row

    def take(p, carry):
        pushes(p).wait()
        stage(back_ref, p)
        return carry

    soon = slots - late_ref.shape[0]
    first = -(-soon // pitch)
    stage(back_ref, mine)
    lax.fori_loop(0, mine, take, 0)
    lax.fori_loop(mine + 1, first, take, 0)
    size = SPREAD if lines % SPREAD == 0 else lines
    batch = staged_ref[:soon, :].astype(BF16)

    def returned(n, carry):
        at = pl.ds(pl.multiple_of(n * size, size), size)
        named = jnp.where(iota((size, soon), 0) + n * size == names_ref[:, :soon], 1.0, 0.0).astype(BF16)
        total = dot(named, batch, 1, 0)
        for c in range(3):
            fluid_ref[c, at, :] = fluid_ref[c, at, :] + total[:, c * span : (c + 1) * span]
        return carry

    lax.fori_loop(0, lines // size, returned, 0)
    lax.fori_loop(first, devices, take, 0)
    late_ref[...] = staged_ref[soon:, :].astype(BF16)
    late_index_ref[...] = names_ref[:, soon:]


def add_kernel(fluid_ref, late_ref, late_index_ref, moved_ref, out_hbm, moved_out, out_ref, out_sem):
    lines, span = fluid_ref.shape[1:]
    size = lines // out_sem.shape[0]
    width = late_ref.shape[0]

    def leave(n):
        at = pl.ds(pl.multiple_of(n * size, size), size)
        return pltpu.make_async_copy(out_ref.at[:, at, :], out_hbm.at[:, at, :], out_sem.at[n])

    def one(n, carry):
        named = jnp.where(iota((size, width), 0) + n * size == late_index_ref[...], 1.0, 0.0).astype(BF16)
        total = dot(named, late_ref[...], 1, 0)
        at = pl.ds(pl.multiple_of(n * size, size), size)
        for c in range(3):
            out_ref[c, at, :] = fluid_ref[c, at, :] + total[:, c * span : (c + 1) * span]
        leave(n).start()
        return carry

    lax.fori_loop(0, lines // size, one, 0)
    moved_out[...] = moved_ref[...]

    def finish(n, carry):
        leave(n).wait()
        return carry

    lax.fori_loop(0, lines // size, finish, 0)


def vmem():
    return pl.BlockSpec(memory_space=pltpu.VMEM)


def smem():
    return pl.BlockSpec(memory_space=pltpu.SMEM)


def hbm():
    return pl.BlockSpec(memory_space=pltpu.HBM)


def params():
    return pltpu.CompilerParams(vmem_limit_bytes=VMEM_LIMIT)


def cost(flops, nbytes):
    return pl.CostEstimate(flops=int(flops), bytes_accessed=int(nbytes), transcendentals=0)


def in_hbm(array):
    return pltpu.with_memory_space_constraint(array, pltpu.HBM)


def shards(velocity_field, interp_weight, particle_velocity, tile_owner, tile_index, block_count):
    _, slab, wall, span = velocity_field.shape
    shape = jax.ShapeDtypeStruct
    gx, gz = lax.axis_size("gx"), lax.axis_size("gz")
    devices = gx * gz
    requests = tile_index.shape[0]
    blocks, particles, cells = interp_weight.shape
    kt = requests // blocks
    pitch = -(-max(2, 3 * requests // devices) // 8) * 8
    slots = devices * pitch
    field_bytes = velocity_field.size * 4

    window = WINDOW if slab % WINDOW == 0 else slab
    lines = slab * wall
    dma = pltpu.SemaphoreType.DMA
    width = slots - 256
    fluid, late, late_index, moved = pl.pallas_call(
        functools.partial(step_kernel, (gx, gz, kt, window)),
        out_shape=(
            pltpu.VMEM((3, lines, span), F32),
            pltpu.VMEM((width, 3 * span), BF16),
            pltpu.VMEM((1, width), jnp.int32),
            pltpu.VMEM(particle_velocity.shape, F32),
        ),
        in_specs=[hbm(), hbm(), smem(), hbm(), hbm(), hbm()],
        out_specs=(vmem(),) * 4,
        scratch_shapes=[
            pltpu.VMEM((1, requests), jnp.int32),
            pltpu.VMEM((1, requests), jnp.int32),
            pltpu.VMEM(particle_velocity.shape, F32),
            pltpu.VMEM((devices, pitch, 3 * span), BF16),
            pltpu.VMEM((devices, 1, 128), jnp.int32),
            pltpu.VMEM((1, slots), jnp.int32),
            pltpu.VMEM((3, lines, span), F32),
            pltpu.VMEM(interp_weight.shape, BF16),
            pltpu.VMEM((blocks // 2, cells, 2 * particles), BF16),
            pltpu.VMEM((devices, 128), jnp.int32),
            pltpu.VMEM((devices, 1, 128), jnp.int32),
            pltpu.SMEM((devices, 1, 128), jnp.int32),
            pltpu.VMEM((requests, 1), jnp.int32),
            pltpu.VMEM((1, requests), jnp.int32),
            pltpu.VMEM((3, pitch, span), F32),
            pltpu.VMEM((devices, pitch, 3 * span), BF16),
            pltpu.VMEM((devices, pitch, 3 * span), BF16),
            pltpu.VMEM((slots, 3 * span), F32),
            pltpu.VMEM((3, blocks, cells), F32),
            pltpu.VMEM((requests, 3 * span), F32),
            pltpu.VMEM((devices, pitch, 3 * span), BF16),
            pltpu.VMEM((3, 1, lines), F32),
            pltpu.VMEM((3, 1, lines), F32),
            pltpu.VMEM((9, wall, span), F32),
            pltpu.VMEM((9, wall, span), F32),
            pltpu.VMEM((3, 1, lines), F32),
            pltpu.VMEM((3, 1, lines), F32),
            pltpu.VMEM((9, wall, span), F32),
            pltpu.VMEM((9, wall, span), F32),
            dma((3,)),
            dma,
            dma,
            dma,
            dma((devices,)),
            dma((devices,)),
            dma((devices,)),
            dma((devices,)),
            dma((devices,)),
            dma((devices,)),
            dma((4,)),
            dma((4,)),
        ],
        compiler_params=pltpu.CompilerParams(
            vmem_limit_bytes=VMEM_LIMIT, collective_id=0, has_side_effects=True
        ),
        cost_estimate=cost(5e8, field_bytes + interp_weight.size * 2),
        name="step",
    )(
        in_hbm(tile_owner.reshape(1, requests)),
        in_hbm(tile_index.reshape(1, requests)),
        block_count,
        in_hbm(particle_velocity),
        in_hbm(velocity_field.reshape(3, lines, span)),
        in_hbm(interp_weight),
    )

    result, moved = pl.pallas_call(
        add_kernel,
        out_shape=(shape((3, lines, span), F32), shape(particle_velocity.shape, F32)),
        in_specs=[vmem()] * 4,
        out_specs=(hbm(), vmem()),
        scratch_shapes=[pltpu.VMEM((3, lines, span), F32), dma((PIECES if lines % (8 * PIECES) == 0 else 1,))],
        compiler_params=params(),
        cost_estimate=cost(2.0 * lines * width * 3 * span, field_bytes * 2),
        name="feedback",
    )(fluid, late, late_index, moved)
    return (result.reshape(velocity_field.shape), moved)


def solution(mesh):
    placed = (
        P(None, "gx", None, "gz"),
        P(("gx", "gz"), None, None),
        P(None, ("gx", "gz"), None),
        P(("gx", "gz"), None),
        P(("gx", "gz")),
        P(("gx", "gz")),
    )
    return jax.shard_map(
        shards,
        mesh=mesh,
        in_specs=placed,
        out_specs=(P(None, "gx", None, "gz"), P(None, ("gx", "gz"), None)),
        check_vma=False,
    )
```

```python
import functools
import math

import jax
import jax.numpy as jnp
from jax import lax
from jax.experimental import pallas as pl
from jax.experimental.pallas import tpu as pltpu
from jax.sharding import PartitionSpec as P

ROOT = (math.sqrt(5.0) / 3.0 - 1.0) * 1.5
GREEN_GAIN = 3.0 / math.sqrt(5.0)
GAMMA = (25.0 / 36.0) * GREEN_GAIN * (1.0 - ROOT * ROOT)
EPS = (1.0 / 12.0) / GAMMA
VISCOSITY = 0.2
RELAX_TIME = 1.0
TIME_STEP = 0.5
LOADING = 0.5
WINDOW = 48
EARLY = 1
CURVE = 1536
CURVE_EARLY = 1
SPREAD = 2048
PIECES = 6
F32 = jnp.float32
BF16 = jnp.bfloat16
VMEM_LIMIT = 40 * 1024 * 1024


def iota(shape, dim):
    return lax.broadcasted_iota(jnp.int32, shape, dim)


def dot(a, b, ca, cb):
    return lax.dot_general(a, b, (((ca,), (cb,)), ((), ())), preferred_element_type=F32)


def end_lanes(span):
    corner = (8, span)
    first = (iota(corner, 0) == 0) & (iota(corner, 1) == 0)
    second = (iota(corner, 0) == 1) & (iota(corner, 1) == span - 1)
    return jnp.where(first | second, 1.0, 0.0)


def halo_lanes(span):
    shape = (8, 3 * span)
    row, lane = iota(shape, 0), iota(shape, 1)
    first = (row == lane // span) & (lane % span == 0)
    last = (row == lane // span + 3) & (lane % span == span - 1)
    return jnp.where(first | last, 1.0, 0.0).astype(BF16)


def second_difference(span):
    shape = (2 * span, span)
    row, lane = iota(shape, 0) % span, iota(shape, 1)
    beside = (row == lane + 1) | (row + 1 == lane)
    return jnp.where(row == lane, -2.0, jnp.where(beside, 1.0, 0.0)).astype(BF16)


def request_slots(kt, pitch, gx, gz, x, z, owner_row, index_row):
    count, devices = owner_row.shape[1], gx * gz
    blocks = count // kt
    r = iota((count, 1), 0)
    cols = iota((count, count), 1)
    pick = cols == kt * (r % blocks) + r // blocks
    owner = jnp.sum(jnp.where(pick, owner_row, 0), 1, keepdims=True)
    index = jnp.sum(jnp.where(pick, index_row, 0), 1, keepdims=True)
    away = (owner // gz + (gx - x)) % gx - gx // 2
    turn = jnp.where(away > 0, 2 * away, jnp.where(away < 0, -2 * away - 1, 0))
    order = (gx - 1 - turn) * gz + (owner % gz + (2 * gz - z - 1)) % gz
    onehot = (order == iota((count, devices), 1)).astype(F32)
    lower = (cols <= r).astype(F32).astype(BF16)
    turned = onehot.astype(BF16)
    seen = dot(lower, turned, 1, 0)
    position = jnp.sum(seen * onehot, 1, keepdims=True).astype(jnp.int32) - 1
    slot = order * pitch + position
    place = slot % 128 == iota((count, 128), 1)
    high = jnp.where(place, (index // 128).astype(F32), 0.0).astype(BF16)
    low = jnp.where(place, (index % 128).astype(F32), 0.0).astype(BF16)
    high_sum, low_sum = dot(turned, high, 0, 0), dot(turned, low, 0, 0)
    send = high_sum.astype(jnp.int32) * 128 + low_sum.astype(jnp.int32)
    return slot, send


def advance(fields, carry):
    state, before = carry[:6], carry[6:]
    parts = [EPS * f + s for f, s in zip(before, state)]
    sums = [parts[3 + c] + fields[0] * parts[c] for c in range(3)]
    moved = [f + ROOT * s for f, s in zip(fields, state)]
    return sums, tuple(moved) + tuple(fields)


def step_kernel(
    sizes, owner_hbm, index_hbm, live_ref, velocity_hbm, field_hbm, weight_hbm,
    fluid_ref, late_ref, late_index_ref, moved_ref,
    owner_ref, index_ref, velocity_ref, back_ref, got_ref, names_ref, field_ref, weight_ref, turned_ref, table_ref, send_ref, got_smem, slot_ref, slot_row_ref, rows_ref, tile_ref, reply_ref,
    staged_ref, own_ref, push_ref, outgoing_ref,
    my_low, my_high, my_left, my_right, low_ref, high_ref, left_ref, right_ref,
    input_sem, field_sem, weight_sem, smem_sem, send_sem, recv_sem, tile_send, tile_recv, back_send, back_recv, edge_send, edge_recv,
):
    gx, gz, kt, window = sizes
    devices = gx * gz
    wall, span = my_left.shape[1:]
    lines = field_ref.shape[1]
    slab = lines // wall
    pitch = tile_ref.shape[1]
    slots = devices * pitch
    x, z = lax.axis_index("gx"), lax.axis_index("gz")
    inputs = [
        pltpu.make_async_copy(src, dst, input_sem.at[k])
        for k, (src, dst) in enumerate(((owner_hbm, owner_ref), (index_hbm, index_ref), (velocity_hbm, velocity_ref)))
    ]
    inputs[0].start()
    inputs[1].start()
    fetch = pltpu.make_async_copy(field_hbm, field_ref, field_sem)
    fetch_weight = pltpu.make_async_copy(weight_hbm, weight_ref, weight_sem)

    barrier = pltpu.get_barrier_semaphore()

    def peer(p, way):
        j = gx - 1 - p // gz
        dx = gx // 2 + (1 - 2 * (j % 2)) * ((j + 1) // 2)
        dz = p % gz + 1
        return lax.rem(x + way * dx + 2 * gx, gx), lax.rem(z + way * dz + 2 * gz, gz)

    mine = gz - 1

    def each(body, start=0, stop=devices):
        def one(u, carry):
            t = u // gz
            t = (1 - t % 2) * (t // 2) + t % 2 * (gx - 1 - t // 2)
            body(t * gz + u % gz)
            return carry

        if start <= mine:
            lax.fori_loop(start, mine, one, 0)
            start = mine + 1
        lax.fori_loop(start, stop, one, 0)

    def greet(p):
        pl.semaphore_signal(barrier, inc=1, device_id=peer(p, 1), device_id_type=pl.DeviceIdType.MESH)

    each(greet)
    fetch.start()
    inputs[0].wait()
    inputs[1].wait()
    slot, send = request_slots(kt, pitch, gx, gz, x, z, owner_ref[...], index_ref[...])
    slot_ref[...] = slot
    table_ref[...] = send
    for d in range(devices):
        send_ref[d] = table_ref[d : d + 1, :]
    pl.semaphore_wait(barrier, devices - 1)

    def exchange(src, dst, sent, got, way):
        def at(p):
            return pltpu.make_async_remote_copy(
                src_ref=src.at[p],
                dst_ref=dst.at[p],
                send_sem=sent.at[p],
                recv_sem=got.at[p],
                device_id=peer(p, way),
                device_id_type=pl.DeviceIdType.MESH,
            )

        return at

    parcel = exchange(send_ref, got_ref, send_sem, recv_sem, 1)
    tiles = exchange(tile_ref, reply_ref, tile_send, tile_recv, -1)
    pushes = exchange(outgoing_ref, back_ref, back_send, back_recv, 1)

    each(lambda n: parcel(n).start())
    got_ref[mine] = send_ref[mine]
    fetch.wait()
    fetch_weight.start()
    inputs[2].start()

    def edge(k, src, dst, peer):
        return pltpu.make_async_remote_copy(
            src_ref=src,
            dst_ref=dst,
            send_sem=edge_send.at[k],
            recv_sem=edge_recv.at[k],
            device_id=peer,
            device_id_type=pl.DeviceIdType.MESH,
        )

    edges = [
        edge(0, my_right, left_ref, (lax.rem(x + 1, gx), z)),
        edge(1, my_left, right_ref, (lax.rem(x + gx - 1, gx), z)),
        edge(2, my_high, low_ref, (x, lax.rem(z + 1, gz))),
        edge(3, my_low, high_ref, (x, lax.rem(z + gz - 1, gz))),
    ]

    def line(i):
        return pl.ds(pl.multiple_of(i * wall, wall), wall)

    def load(i):
        u = [field_ref[c, line(i), :] for c in range(3)]
        return u + [u[0] * u[c] for c in range(3)]

    zero = jnp.zeros((wall, span), F32)

    def moments(order):
        def one(i, state):
            return tuple(f + ROOT * s for f, s in zip(load(order(i)), state))

        return lax.fori_loop(0, window, one, (zero,) * 6, unroll=4)

    for k, value in enumerate(moments(lambda i: slab - window + i)):
        my_right[k] = value
    for c in range(3):
        my_right[6 + c] = field_ref[c, lines - wall :, :]
    edges[0].start()
    for k, value in enumerate(moments(lambda i: window - 1 - i)):
        my_left[k] = value
    for c in range(3):
        my_left[6 + c] = field_ref[c, :wall, :]
    edges[1].start()

    def up(i, carry):
        sums, carry = advance(load(i), carry)
        for c in range(3):
            fluid_ref[c, line(i), :] = 0.5 * GAMMA * sums[c]
        return carry

    ends = end_lanes(span).astype(BF16)
    span_rows = window
    for c in range(3):
        for n in range(slab // span_rows):
            part = slice(n * span_rows * wall, (n + 1) * span_rows * wall)
            lanes = dot(ends, field_ref[c, part].astype(BF16), 1, 1)
            my_low[c, :, part] = lanes[0:1]
            my_high[c, :, part] = lanes[1:2]
    edges[2].start()
    edges[3].start()
    early = slab * EARLY // 8
    carry = lax.fori_loop(0, early, up, (zero,) * 12, unroll=4)

    each(lambda n: parcel(n).wait())
    copy = pltpu.make_async_copy(got_ref, got_smem, smem_sem)
    copy.start()
    copy.wait()

    def collect(p):
        for k in range(pitch):
            row = jnp.minimum(jnp.maximum(got_smem[p, 0, lax.rem(p * pitch + k, 128)], 0), lines - 1)
            for c in range(3):
                rows_ref[c, k : k + 1, :] = field_ref[c, pl.ds(row, 1), :]
        for c in range(3):
            tile_ref[p, :, c * span : (c + 1) * span] = rows_ref[c].astype(BF16)

    def gather(p):
        collect(p)
        tiles(p).start()

    each(gather)
    collect(mine)
    reply_ref[mine] = tile_ref[mine]

    lax.fori_loop(early, slab, up, carry, unroll=4)

    particles, cells = weight_ref.shape[1:]
    fetch_weight.wait()

    def turn(n, carry):
        for b in range(2):
            turned_ref[n, :, b * particles : (b + 1) * particles] = jnp.transpose(weight_ref[2 * n + b])
        return carry

    lax.fori_loop(0, turned_ref.shape[0], turn, 0)
    edges[2].wait()
    edges[3].wait()
    long = CURVE if lines % CURVE == 0 else lines
    pick, curl = halo_lanes(span), second_difference(span)

    def curve(n, carry):
        at = pl.ds(pl.multiple_of(n * long, long), long)
        row = iota((8, long), 0)
        halo = jnp.zeros((8, long), F32)
        for c in range(3):
            halo = jnp.where(row == c, low_ref[c, :, at], jnp.where(row == c + 3, high_ref[c, :, at], halo))
        halo = dot(halo.astype(BF16), pick, 0, 0)
        for c in range(3):
            u = field_ref[c, at, :]
            head = u.astype(BF16)
            rest = (u - head.astype(F32)).astype(BF16)
            inside = dot(jnp.concatenate([head, rest], 1), curl, 1, 0)
            total = inside + halo[:, c * span : (c + 1) * span]
            fluid_ref[c, at, :] = fluid_ref[c, at, :] + VISCOSITY * total
        return carry

    half_way = lines // long * CURVE_EARLY // 4
    lax.fori_loop(0, half_way, curve, 0)

    count = slot_ref.shape[0]
    same = iota((count, count), 0) == iota((count, count), 1)
    slot_row_ref[...] = jnp.sum(jnp.where(same, slot_ref[...], 0), 0, keepdims=True)

    def stage(src, p):
        staged_ref[pl.ds(pl.multiple_of(p * pitch, pitch), pitch), :] = src[p].astype(F32)

    stage(reply_ref, mine)

    def receive(p):
        tiles(p).wait()
        stage(reply_ref, p)

    each(receive)

    blocks = count // kt
    chosen = jnp.where(slot_ref[...] == iota((count, slots), 1), 1.0, 0.0).astype(BF16)
    own = dot(chosen, staged_ref[...].astype(BF16), 1, 0)
    for j in range(kt):
        for c in range(3):
            own_ref[c, :, j * span : (j + 1) * span] = own[j * blocks : (j + 1) * blocks, c * span : (c + 1) * span]
    inputs[2].wait()
    group = 16 if blocks % 16 == 0 else 8
    live_blocks = live_ref[0]

    def particle(step, carry):
        base = pl.multiple_of(step * group, group)
        tile = jnp.concatenate([own_ref[c, pl.ds(base, group), :] for c in range(3)], 0).astype(BF16)
        row = iota((3 * group, particles), 0) % group
        sampled = jnp.zeros((3 * group, particles), F32)
        for b in range(0, group, 2):
            both = dot(tile, turned_ref[base // 2 + b // 2], 1, 0)
            sampled = jnp.where(row == b, both[:, :particles], sampled)
            sampled = jnp.where(row == b + 1, both[:, particles:], sampled)
        velocity = jnp.concatenate([velocity_ref[c, pl.ds(base, group), :] for c in range(3)], 0)
        live = jnp.where(row + base < live_blocks, 1.0, 0.0)
        drag = live * (sampled - velocity) * (1.0 / RELAX_TIME)
        moved = velocity + TIME_STEP * drag
        for c in range(3):
            moved_ref[c, pl.ds(base, group), :] = moved[c * group : (c + 1) * group]
        half = drag.astype(BF16)
        row = iota((3 * group, cells), 0) % group
        push = jnp.zeros((3 * group, cells), F32)
        for b in range(group):
            push = jnp.where(row == b, dot(half, weight_ref[base + b], 1, 0), push)
        push = -LOADING * push
        for j in range(kt):
            for c in range(3):
                push_ref[pl.ds(j * blocks + base, group), c * span : (c + 1) * span] = push[
                    c * group : (c + 1) * group, j * span : (j + 1) * span
                ]
        return carry

    lax.fori_loop(0, blocks // group, particle, 0, unroll=True)

    pushed = push_ref[...].astype(BF16)
    lot = 8
    chunks = devices // lot
    for q in sorted(range(chunks), key=lambda q: min(q, chunks - 1 - q)):
        named = jnp.where(iota((lot * pitch, count), 0) + q * lot * pitch == slot_row_ref[...], 1.0, 0.0).astype(BF16)
        placed = dot(named, pushed, 1, 0)
        for p in range(lot):
            outgoing_ref[q * lot + p] = placed[p * pitch : (p + 1) * pitch].astype(BF16)
        if q >= chunks // 2:
            ready = chunks - q
            each(lambda p: pushes(p).start(), 2 * lot * (ready - 1), 2 * lot * ready)
    back_ref[mine] = outgoing_ref[mine]

    def down(n, carry):
        i = slab - 1 - n
        sums, carry = advance(load(i), carry)
        for c in range(3):
            fluid_ref[c, line(i), :] = fluid_ref[c, line(i), :] - 0.5 * GAMMA * sums[c]
        return carry

    lax.fori_loop(0, slab, down, (zero,) * 12, unroll=4)

    def border(ref):
        u = [ref[6 + c] for c in range(3)]
        return [ref[k] for k in range(6)], u + [u[0] * u[c] for c in range(3)]

    def spread(ref, gain, order):
        state, before = border(ref)

        def add(i, parts):
            u0 = field_ref[0, line(i), :]
            for c in range(3):
                fluid_ref[c, line(i), :] = fluid_ref[c, line(i), :] + gain * (parts[3 + c] + u0 * parts[c])

        add(order(0), [EPS * f + s for f, s in zip(before, state)])

        def one(n, state):
            add(order(n), state)
            return tuple(ROOT * s for s in state)

        lax.fori_loop(1, window, one, tuple(ROOT * s for s in state), unroll=2)

    edges[0].wait()
    spread(left_ref, 0.5 * GAMMA, lambda n: n)
    edges[1].wait()
    spread(right_ref, -0.5 * GAMMA, lambda n: slab - 1 - n)

    lax.fori_loop(half_way, lines // long, curve, 0)
    for g in range(slots // 128):
        row = jnp.zeros((1, 128), jnp.int32)
        for p in range(g * 128 // pitch, min(devices, (g * 128 + 127) // pitch + 1)):
            flat = iota((1, 128), 1) + (g * 128 - p * pitch)
            row = jnp.where((flat >= 0) & (flat < pitch), got_ref[p], row)
        names_ref[:, g * 128 : (g + 1) * 128] = row

    def take(p, carry):
        pushes(p).wait()
        stage(back_ref, p)
        return carry

    soon = slots - late_ref.shape[0]
    first = -(-soon // pitch)
    stage(back_ref, mine)
    lax.fori_loop(0, mine, take, 0)
    lax.fori_loop(mine + 1, first, take, 0)
    size = SPREAD if lines % SPREAD == 0 else lines
    batch = staged_ref[:soon, :].astype(BF16)

    def returned(n, carry):
        at = pl.ds(pl.multiple_of(n * size, size), size)
        named = jnp.where(iota((size, soon), 0) + n * size == names_ref[:, :soon], 1.0, 0.0).astype(BF16)
        total = dot(named, batch, 1, 0)
        for c in range(3):
            fluid_ref[c, at, :] = fluid_ref[c, at, :] + total[:, c * span : (c + 1) * span]
        return carry

    lax.fori_loop(0, lines // size, returned, 0)
    lax.fori_loop(first, devices, take, 0)
    late_ref[...] = staged_ref[soon:, :].astype(BF16)
    late_index_ref[...] = names_ref[:, soon:]


def add_kernel(fluid_ref, late_ref, late_index_ref, moved_ref, out_hbm, moved_out, out_ref, out_sem):
    lines, span = fluid_ref.shape[1:]
    size = lines // out_sem.shape[0]
    width = late_ref.shape[0]

    def leave(n):
        at = pl.ds(pl.multiple_of(n * size, size), size)
        return pltpu.make_async_copy(out_ref.at[:, at, :], out_hbm.at[:, at, :], out_sem.at[n])

    def one(n, carry):
        named = jnp.where(iota((size, width), 0) + n * size == late_index_ref[...], 1.0, 0.0).astype(BF16)
        total = dot(named, late_ref[...], 1, 0)
        at = pl.ds(pl.multiple_of(n * size, size), size)
        for c in range(3):
            out_ref[c, at, :] = fluid_ref[c, at, :] + total[:, c * span : (c + 1) * span]
        leave(n).start()
        return carry

    lax.fori_loop(0, lines // size, one, 0)
    moved_out[...] = moved_ref[...]

    def finish(n, carry):
        leave(n).wait()
        return carry

    lax.fori_loop(0, lines // size, finish, 0)


def vmem():
    return pl.BlockSpec(memory_space=pltpu.VMEM)


def smem():
    return pl.BlockSpec(memory_space=pltpu.SMEM)


def hbm():
    return pl.BlockSpec(memory_space=pltpu.HBM)


def params():
    return pltpu.CompilerParams(vmem_limit_bytes=VMEM_LIMIT)


def cost(flops, nbytes):
    return pl.CostEstimate(flops=int(flops), bytes_accessed=int(nbytes), transcendentals=0)


def in_hbm(array):
    return pltpu.with_memory_space_constraint(array, pltpu.HBM)


def shards(velocity_field, interp_weight, particle_velocity, tile_owner, tile_index, block_count):
    _, slab, wall, span = velocity_field.shape
    shape = jax.ShapeDtypeStruct
    gx, gz = lax.axis_size("gx"), lax.axis_size("gz")
    devices = gx * gz
    requests = tile_index.shape[0]
    blocks, particles, cells = interp_weight.shape
    kt = requests // blocks
    pitch = -(-max(2, 3 * requests // devices) // 8) * 8
    slots = devices * pitch
    field_bytes = velocity_field.size * 4

    window = WINDOW if slab % WINDOW == 0 else slab
    lines = slab * wall
    dma = pltpu.SemaphoreType.DMA
    width = slots - 256
    fluid, late, late_index, moved = pl.pallas_call(
        functools.partial(step_kernel, (gx, gz, kt, window)),
        out_shape=(
            pltpu.VMEM((3, lines, span), F32),
            pltpu.VMEM((width, 3 * span), BF16),
            pltpu.VMEM((1, width), jnp.int32),
            pltpu.VMEM(particle_velocity.shape, F32),
        ),
        in_specs=[hbm(), hbm(), smem(), hbm(), hbm(), hbm()],
        out_specs=(vmem(),) * 4,
        scratch_shapes=[
            pltpu.VMEM((1, requests), jnp.int32),
            pltpu.VMEM((1, requests), jnp.int32),
            pltpu.VMEM(particle_velocity.shape, F32),
            pltpu.VMEM((devices, pitch, 3 * span), BF16),
            pltpu.VMEM((devices, 1, 128), jnp.int32),
            pltpu.VMEM((1, slots), jnp.int32),
            pltpu.VMEM((3, lines, span), F32),
            pltpu.VMEM(interp_weight.shape, BF16),
            pltpu.VMEM((blocks // 2, cells, 2 * particles), BF16),
            pltpu.VMEM((devices, 128), jnp.int32),
            pltpu.VMEM((devices, 1, 128), jnp.int32),
            pltpu.SMEM((devices, 1, 128), jnp.int32),
            pltpu.VMEM((requests, 1), jnp.int32),
            pltpu.VMEM((1, requests), jnp.int32),
            pltpu.VMEM((3, pitch, span), F32),
            pltpu.VMEM((devices, pitch, 3 * span), BF16),
            pltpu.VMEM((devices, pitch, 3 * span), BF16),
            pltpu.VMEM((slots, 3 * span), F32),
            pltpu.VMEM((3, blocks, cells), F32),
            pltpu.VMEM((requests, 3 * span), F32),
            pltpu.VMEM((devices, pitch, 3 * span), BF16),
            pltpu.VMEM((3, 1, lines), F32),
            pltpu.VMEM((3, 1, lines), F32),
            pltpu.VMEM((9, wall, span), F32),
            pltpu.VMEM((9, wall, span), F32),
            pltpu.VMEM((3, 1, lines), F32),
            pltpu.VMEM((3, 1, lines), F32),
            pltpu.VMEM((9, wall, span), F32),
            pltpu.VMEM((9, wall, span), F32),
            dma((3,)),
            dma,
            dma,
            dma,
            dma((devices,)),
            dma((devices,)),
            dma((devices,)),
            dma((devices,)),
            dma((devices,)),
            dma((devices,)),
            dma((4,)),
            dma((4,)),
        ],
        compiler_params=pltpu.CompilerParams(
            vmem_limit_bytes=VMEM_LIMIT, collective_id=0, has_side_effects=True
        ),
        cost_estimate=cost(5e8, field_bytes + interp_weight.size * 2),
        name="step",
    )(
        in_hbm(tile_owner.reshape(1, requests)),
        in_hbm(tile_index.reshape(1, requests)),
        block_count,
        in_hbm(particle_velocity),
        in_hbm(velocity_field.reshape(3, lines, span)),
        in_hbm(interp_weight),
    )

    result, moved = pl.pallas_call(
        add_kernel,
        out_shape=(shape((3, lines, span), F32), shape(particle_velocity.shape, F32)),
        in_specs=[vmem()] * 4,
        out_specs=(hbm(), vmem()),
        scratch_shapes=[pltpu.VMEM((3, lines, span), F32), dma((PIECES if lines % (8 * PIECES) == 0 else 1,))],
        compiler_params=params(),
        cost_estimate=cost(2.0 * lines * width * 3 * span, field_bytes * 2),
        name="feedback",
    )(fluid, late, late_index, moved)
    return (result.reshape(velocity_field.shape), moved)


def solution(mesh):
    placed = (
        P(None, "gx", None, "gz"),
        P(("gx", "gz"), None, None),
        P(None, ("gx", "gz"), None),
        P(("gx", "gz"), None),
        P(("gx", "gz")),
        P(("gx", "gz")),
    )
    return jax.shard_map(
        shards,
        mesh=mesh,
        in_specs=placed,
        out_specs=(P(None, "gx", None, "gz"), P(None, ("gx", "gz"), None)),
        check_vma=False,
    )
```

```python
import functools
import math

import jax
import jax.numpy as jnp
from jax import lax
from jax.experimental import pallas as pl
from jax.experimental.pallas import tpu as pltpu
from jax.sharding import PartitionSpec as P

ROOT = (math.sqrt(5.0) / 3.0 - 1.0) * 1.5
GREEN_GAIN = 3.0 / math.sqrt(5.0)
GAMMA = (25.0 / 36.0) * GREEN_GAIN * (1.0 - ROOT * ROOT)
EPS = (1.0 / 12.0) / GAMMA
VISCOSITY = 0.2
RELAX_TIME = 1.0
TIME_STEP = 0.5
LOADING = 0.5
WINDOW = 48
EARLY = 1
CURVE = 1536
CURVE_EARLY = 1
SPREAD = 2048
PIECES = 6
F32 = jnp.float32
BF16 = jnp.bfloat16
VMEM_LIMIT = 40 * 1024 * 1024


def iota(shape, dim):
    return lax.broadcasted_iota(jnp.int32, shape, dim)


def dot(a, b, ca, cb):
    return lax.dot_general(a, b, (((ca,), (cb,)), ((), ())), preferred_element_type=F32)


def end_lanes(span):
    corner = (8, span)
    first = (iota(corner, 0) == 0) & (iota(corner, 1) == 0)
    second = (iota(corner, 0) == 1) & (iota(corner, 1) == span - 1)
    return jnp.where(first | second, 1.0, 0.0)


def halo_lanes(span):
    shape = (8, 3 * span)
    row, lane = iota(shape, 0), iota(shape, 1)
    first = (row == lane // span) & (lane % span == 0)
    last = (row == lane // span + 3) & (lane % span == span - 1)
    return jnp.where(first | last, 1.0, 0.0).astype(BF16)


def second_difference(span):
    shape = (2 * span, span)
    row, lane = iota(shape, 0) % span, iota(shape, 1)
    beside = (row == lane + 1) | (row + 1 == lane)
    return jnp.where(row == lane, -2.0, jnp.where(beside, 1.0, 0.0)).astype(BF16)


def request_slots(kt, pitch, gx, gz, x, z, owner_row, index_row):
    count, devices = owner_row.shape[1], gx * gz
    blocks = count // kt
    r = iota((count, 1), 0)
    cols = iota((count, count), 1)
    pick = cols == kt * (r % blocks) + r // blocks
    owner = jnp.sum(jnp.where(pick, owner_row, 0), 1, keepdims=True)
    index = jnp.sum(jnp.where(pick, index_row, 0), 1, keepdims=True)
    away = (owner // gz + (gx - x)) % gx - gx // 2
    turn = jnp.where(away > 0, 2 * away, jnp.where(away < 0, -2 * away - 1, 0))
    order = (gx - 1 - turn) * gz + (owner % gz + (2 * gz - z - 1)) % gz
    onehot = (order == iota((count, devices), 1)).astype(F32)
    lower = (cols <= r).astype(F32).astype(BF16)
    turned = onehot.astype(BF16)
    seen = dot(lower, turned, 1, 0)
    position = jnp.sum(seen * onehot, 1, keepdims=True).astype(jnp.int32) - 1
    slot = order * pitch + position
    place = slot % 128 == iota((count, 128), 1)
    high = jnp.where(place, (index // 128).astype(F32), 0.0).astype(BF16)
    low = jnp.where(place, (index % 128).astype(F32), 0.0).astype(BF16)
    high_sum, low_sum = dot(turned, high, 0, 0), dot(turned, low, 0, 0)
    send = high_sum.astype(jnp.int32) * 128 + low_sum.astype(jnp.int32)
    return slot, send


def advance(fields, carry):
    state, before = carry[:6], carry[6:]
    parts = [EPS * f + s for f, s in zip(before, state)]
    sums = [parts[3 + c] + fields[0] * parts[c] for c in range(3)]
    moved = [f + ROOT * s for f, s in zip(fields, state)]
    return sums, tuple(moved) + tuple(fields)


def step_kernel(
    sizes, owner_hbm, index_hbm, live_ref, velocity_hbm, field_hbm, weight_hbm,
    fluid_ref, late_ref, late_index_ref, moved_ref,
    owner_ref, index_ref, velocity_ref, back_ref, got_ref, names_ref, field_ref, weight_ref, turned_ref, table_ref, send_ref, got_smem, slot_ref, slot_row_ref, rows_ref, tile_ref, reply_ref,
    staged_ref, own_ref, push_ref, outgoing_ref,
    my_low, my_high, my_left, my_right, low_ref, high_ref, left_ref, right_ref,
    input_sem, field_sem, weight_sem, smem_sem, send_sem, recv_sem, tile_send, tile_recv, back_send, back_recv, edge_send, edge_recv,
):
    gx, gz, kt, window = sizes
    devices = gx * gz
    wall, span = my_left.shape[1:]
    lines = field_ref.shape[1]
    slab = lines // wall
    pitch = tile_ref.shape[1]
    slots = devices * pitch
    x, z = lax.axis_index("gx"), lax.axis_index("gz")
    inputs = [
        pltpu.make_async_copy(src, dst, input_sem.at[k])
        for k, (src, dst) in enumerate(((owner_hbm, owner_ref), (index_hbm, index_ref), (velocity_hbm, velocity_ref)))
    ]
    inputs[0].start()
    inputs[1].start()
    fetch = pltpu.make_async_copy(field_hbm, field_ref, field_sem)
    fetch_weight = pltpu.make_async_copy(weight_hbm, weight_ref, weight_sem)

    barrier = pltpu.get_barrier_semaphore()

    def peer(p, way):
        j = gx - 1 - p // gz
        dx = gx // 2 + (1 - 2 * (j % 2)) * ((j + 1) // 2)
        dz = p % gz + 1
        return lax.rem(x + way * dx + 2 * gx, gx), lax.rem(z + way * dz + 2 * gz, gz)

    mine = gz - 1

    def each(body, start=0, stop=devices):
        def one(u, carry):
            t = u // gz
            t = (1 - t % 2) * (t // 2) + t % 2 * (gx - 1 - t // 2)
            body(t * gz + u % gz)
            return carry

        if start <= mine:
            lax.fori_loop(start, mine, one, 0)
            start = mine + 1
        lax.fori_loop(start, stop, one, 0)

    def greet(p):
        pl.semaphore_signal(barrier, inc=1, device_id=peer(p, 1), device_id_type=pl.DeviceIdType.MESH)

    each(greet)
    fetch.start()
    inputs[0].wait()
    inputs[1].wait()
    slot, send = request_slots(kt, pitch, gx, gz, x, z, owner_ref[...], index_ref[...])
    slot_ref[...] = slot
    table_ref[...] = send
    for d in range(devices):
        send_ref[d] = table_ref[d : d + 1, :]
    pl.semaphore_wait(barrier, devices - 1)

    def exchange(src, dst, sent, got, way):
        def at(p):
            return pltpu.make_async_remote_copy(
                src_ref=src.at[p],
                dst_ref=dst.at[p],
                send_sem=sent.at[p],
                recv_sem=got.at[p],
                device_id=peer(p, way),
                device_id_type=pl.DeviceIdType.MESH,
            )

        return at

    parcel = exchange(send_ref, got_ref, send_sem, recv_sem, 1)
    tiles = exchange(tile_ref, reply_ref, tile_send, tile_recv, -1)
    pushes = exchange(outgoing_ref, back_ref, back_send, back_recv, 1)

    each(lambda n: parcel(n).start())
    got_ref[mine] = send_ref[mine]
    fetch.wait()
    fetch_weight.start()
    inputs[2].start()

    def edge(k, src, dst, peer):
        return pltpu.make_async_remote_copy(
            src_ref=src,
            dst_ref=dst,
            send_sem=edge_send.at[k],
            recv_sem=edge_recv.at[k],
            device_id=peer,
            device_id_type=pl.DeviceIdType.MESH,
        )

    edges = [
        edge(0, my_right, left_ref, (lax.rem(x + 1, gx), z)),
        edge(1, my_left, right_ref, (lax.rem(x + gx - 1, gx), z)),
        edge(2, my_high, low_ref, (x, lax.rem(z + 1, gz))),
        edge(3, my_low, high_ref, (x, lax.rem(z + gz - 1, gz))),
    ]

    def line(i):
        return pl.ds(pl.multiple_of(i * wall, wall), wall)

    def load(i):
        u = [field_ref[c, line(i), :] for c in range(3)]
        return u + [u[0] * u[c] for c in range(3)]

    zero = jnp.zeros((wall, span), F32)

    def moments(order):
        def one(i, state):
            return tuple(f + ROOT * s for f, s in zip(load(order(i)), state))

        return lax.fori_loop(0, window, one, (zero,) * 6, unroll=4)

    for k, value in enumerate(moments(lambda i: slab - window + i)):
        my_right[k] = value
    for c in range(3):
        my_right[6 + c] = field_ref[c, lines - wall :, :]
    edges[0].start()
    for k, value in enumerate(moments(lambda i: window - 1 - i)):
        my_left[k] = value
    for c in range(3):
        my_left[6 + c] = field_ref[c, :wall, :]
    edges[1].start()

    def up(i, carry):
        sums, carry = advance(load(i), carry)
        for c in range(3):
            fluid_ref[c, line(i), :] = 0.5 * GAMMA * sums[c]
        return carry

    ends = end_lanes(span).astype(BF16)
    span_rows = window
    for c in range(3):
        for n in range(slab // span_rows):
            part = slice(n * span_rows * wall, (n + 1) * span_rows * wall)
            lanes = dot(ends, field_ref[c, part].astype(BF16), 1, 1)
            my_low[c, :, part] = lanes[0:1]
            my_high[c, :, part] = lanes[1:2]
    edges[2].start()
    edges[3].start()
    early = slab * EARLY // 8
    carry = lax.fori_loop(0, early, up, (zero,) * 12, unroll=4)

    each(lambda n: parcel(n).wait())
    copy = pltpu.make_async_copy(got_ref, got_smem, smem_sem)
    copy.start()
    copy.wait()

    def collect(p):
        for k in range(pitch):
            row = jnp.minimum(jnp.maximum(got_smem[p, 0, lax.rem(p * pitch + k, 128)], 0), lines - 1)
            for c in range(3):
                rows_ref[c, k : k + 1, :] = field_ref[c, pl.ds(row, 1), :]
        for c in range(3):
            tile_ref[p, :, c * span : (c + 1) * span] = rows_ref[c].astype(BF16)

    def gather(p):
        collect(p)
        tiles(p).start()

    each(gather)
    collect(mine)
    reply_ref[mine] = tile_ref[mine]

    lax.fori_loop(early, slab, up, carry, unroll=4)

    particles, cells = weight_ref.shape[1:]
    fetch_weight.wait()

    def turn(n, carry):
        for b in range(2):
            turned_ref[n, :, b * particles : (b + 1) * particles] = jnp.transpose(weight_ref[2 * n + b])
        return carry

    lax.fori_loop(0, turned_ref.shape[0], turn, 0)
    edges[2].wait()
    edges[3].wait()
    long = CURVE if lines % CURVE == 0 else lines
    pick, curl = halo_lanes(span), second_difference(span)

    def curve(n, carry):
        at = pl.ds(pl.multiple_of(n * long, long), long)
        row = iota((8, long), 0)
        halo = jnp.zeros((8, long), F32)
        for c in range(3):
            halo = jnp.where(row == c, low_ref[c, :, at], jnp.where(row == c + 3, high_ref[c, :, at], halo))
        halo = dot(halo.astype(BF16), pick, 0, 0)
        for c in range(3):
            u = field_ref[c, at, :]
            head = u.astype(BF16)
            rest = (u - head.astype(F32)).astype(BF16)
            inside = dot(jnp.concatenate([head, rest], 1), curl, 1, 0)
            total = inside + halo[:, c * span : (c + 1) * span]
            fluid_ref[c, at, :] = fluid_ref[c, at, :] + VISCOSITY * total
        return carry

    half_way = lines // long * CURVE_EARLY // 4
    lax.fori_loop(0, half_way, curve, 0)

    count = slot_ref.shape[0]
    same = iota((count, count), 0) == iota((count, count), 1)
    slot_row_ref[...] = jnp.sum(jnp.where(same, slot_ref[...], 0), 0, keepdims=True)

    def stage(src, p):
        staged_ref[pl.ds(pl.multiple_of(p * pitch, pitch), pitch), :] = src[p].astype(F32)

    stage(reply_ref, mine)

    def receive(p):
        tiles(p).wait()
        stage(reply_ref, p)

    each(receive)

    blocks = count // kt
    chosen = jnp.where(slot_ref[...] == iota((count, slots), 1), 1.0, 0.0).astype(BF16)
    own = dot(chosen, staged_ref[...].astype(BF16), 1, 0)
    for j in range(kt):
        for c in range(3):
            own_ref[c, :, j * span : (j + 1) * span] = own[j * blocks : (j + 1) * blocks, c * span : (c + 1) * span]
    inputs[2].wait()
    group = 16 if blocks % 16 == 0 else 8
    live_blocks = live_ref[0]

    def particle(step, carry):
        base = pl.multiple_of(step * group, group)
        tile = jnp.concatenate([own_ref[c, pl.ds(base, group), :] for c in range(3)], 0).astype(BF16)
        row = iota((3 * group, particles), 0) % group
        sampled = jnp.zeros((3 * group, particles), F32)
        for b in range(0, group, 2):
            both = dot(tile, turned_ref[base // 2 + b // 2], 1, 0)
            sampled = jnp.where(row == b, both[:, :particles], sampled)
            sampled = jnp.where(row == b + 1, both[:, particles:], sampled)
        velocity = jnp.concatenate([velocity_ref[c, pl.ds(base, group), :] for c in range(3)], 0)
        live = jnp.where(row + base < live_blocks, 1.0, 0.0)
        drag = live * (sampled - velocity) * (1.0 / RELAX_TIME)
        moved = velocity + TIME_STEP * drag
        for c in range(3):
            moved_ref[c, pl.ds(base, group), :] = moved[c * group : (c + 1) * group]
        half = drag.astype(BF16)
        row = iota((3 * group, cells), 0) % group
        push = jnp.zeros((3 * group, cells), F32)
        for b in range(group):
            push = jnp.where(row == b, dot(half, weight_ref[base + b], 1, 0), push)
        push = -LOADING * push
        for j in range(kt):
            for c in range(3):
                push_ref[pl.ds(j * blocks + base, group), c * span : (c + 1) * span] = push[
                    c * group : (c + 1) * group, j * span : (j + 1) * span
                ]
        return carry

    lax.fori_loop(0, blocks // group, particle, 0, unroll=True)

    pushed = push_ref[...].astype(BF16)
    lot = 8
    chunks = devices // lot
    for q in sorted(range(chunks), key=lambda q: min(q, chunks - 1 - q)):
        named = jnp.where(iota((lot * pitch, count), 0) + q * lot * pitch == slot_row_ref[...], 1.0, 0.0).astype(BF16)
        placed = dot(named, pushed, 1, 0)
        for p in range(lot):
            outgoing_ref[q * lot + p] = placed[p * pitch : (p + 1) * pitch].astype(BF16)
        if q >= chunks // 2:
            ready = chunks - q
            each(lambda p: pushes(p).start(), 2 * lot * (ready - 1), 2 * lot * ready)
    back_ref[mine] = outgoing_ref[mine]

    def down(n, carry):
        i = slab - 1 - n
        sums, carry = advance(load(i), carry)
        for c in range(3):
            fluid_ref[c, line(i), :] = fluid_ref[c, line(i), :] - 0.5 * GAMMA * sums[c]
        return carry

    lax.fori_loop(0, slab, down, (zero,) * 12, unroll=4)

    def border(ref):
        u = [ref[6 + c] for c in range(3)]
        return [ref[k] for k in range(6)], u + [u[0] * u[c] for c in range(3)]

    def spread(ref, gain, order):
        state, before = border(ref)

        def add(i, parts):
            u0 = field_ref[0, line(i), :]
            for c in range(3):
                fluid_ref[c, line(i), :] = fluid_ref[c, line(i), :] + gain * (parts[3 + c] + u0 * parts[c])

        add(order(0), [EPS * f + s for f, s in zip(before, state)])

        def one(n, state):
            add(order(n), state)
            return tuple(ROOT * s for s in state)

        lax.fori_loop(1, window, one, tuple(ROOT * s for s in state), unroll=8)

    edges[0].wait()
    spread(left_ref, 0.5 * GAMMA, lambda n: n)
    edges[1].wait()
    spread(right_ref, -0.5 * GAMMA, lambda n: slab - 1 - n)

    lax.fori_loop(half_way, lines // long, curve, 0)
    for g in range(slots // 128):
        row = jnp.zeros((1, 128), jnp.int32)
        for p in range(g * 128 // pitch, min(devices, (g * 128 + 127) // pitch + 1)):
            flat = iota((1, 128), 1) + (g * 128 - p * pitch)
            row = jnp.where((flat >= 0) & (flat < pitch), got_ref[p], row)
        names_ref[:, g * 128 : (g + 1) * 128] = row

    def take(p, carry):
        pushes(p).wait()
        stage(back_ref, p)
        return carry

    soon = slots - late_ref.shape[0]
    first = -(-soon // pitch)
    stage(back_ref, mine)
    lax.fori_loop(0, mine, take, 0)
    lax.fori_loop(mine + 1, first, take, 0)
    size = SPREAD if lines % SPREAD == 0 else lines
    batch = staged_ref[:soon, :].astype(BF16)

    def returned(n, carry):
        at = pl.ds(pl.multiple_of(n * size, size), size)
        named = jnp.where(iota((size, soon), 0) + n * size == names_ref[:, :soon], 1.0, 0.0).astype(BF16)
        total = dot(named, batch, 1, 0)
        for c in range(3):
            fluid_ref[c, at, :] = fluid_ref[c, at, :] + total[:, c * span : (c + 1) * span]
        return carry

    lax.fori_loop(0, lines // size, returned, 0)
    lax.fori_loop(first, devices, take, 0)
    late_ref[...] = staged_ref[soon:, :].astype(BF16)
    late_index_ref[...] = names_ref[:, soon:]


def add_kernel(fluid_ref, late_ref, late_index_ref, moved_ref, out_hbm, moved_out, out_ref, out_sem):
    lines, span = fluid_ref.shape[1:]
    size = lines // out_sem.shape[0]
    width = late_ref.shape[0]

    def leave(n):
        at = pl.ds(pl.multiple_of(n * size, size), size)
        return pltpu.make_async_copy(out_ref.at[:, at, :], out_hbm.at[:, at, :], out_sem.at[n])

    def one(n, carry):
        named = jnp.where(iota((size, width), 0) + n * size == late_index_ref[...], 1.0, 0.0).astype(BF16)
        total = dot(named, late_ref[...], 1, 0)
        at = pl.ds(pl.multiple_of(n * size, size), size)
        for c in range(3):
            out_ref[c, at, :] = fluid_ref[c, at, :] + total[:, c * span : (c + 1) * span]
        leave(n).start()
        return carry

    lax.fori_loop(0, lines // size, one, 0)
    moved_out[...] = moved_ref[...]

    def finish(n, carry):
        leave(n).wait()
        return carry

    lax.fori_loop(0, lines // size, finish, 0)


def vmem():
    return pl.BlockSpec(memory_space=pltpu.VMEM)


def smem():
    return pl.BlockSpec(memory_space=pltpu.SMEM)


def hbm():
    return pl.BlockSpec(memory_space=pltpu.HBM)


def params():
    return pltpu.CompilerParams(vmem_limit_bytes=VMEM_LIMIT)


def cost(flops, nbytes):
    return pl.CostEstimate(flops=int(flops), bytes_accessed=int(nbytes), transcendentals=0)


def in_hbm(array):
    return pltpu.with_memory_space_constraint(array, pltpu.HBM)


def shards(velocity_field, interp_weight, particle_velocity, tile_owner, tile_index, block_count):
    _, slab, wall, span = velocity_field.shape
    shape = jax.ShapeDtypeStruct
    gx, gz = lax.axis_size("gx"), lax.axis_size("gz")
    devices = gx * gz
    requests = tile_index.shape[0]
    blocks, particles, cells = interp_weight.shape
    kt = requests // blocks
    pitch = -(-max(2, 3 * requests // devices) // 8) * 8
    slots = devices * pitch
    field_bytes = velocity_field.size * 4

    window = WINDOW if slab % WINDOW == 0 else slab
    lines = slab * wall
    dma = pltpu.SemaphoreType.DMA
    width = slots - 256
    fluid, late, late_index, moved = pl.pallas_call(
        functools.partial(step_kernel, (gx, gz, kt, window)),
        out_shape=(
            pltpu.VMEM((3, lines, span), F32),
            pltpu.VMEM((width, 3 * span), BF16),
            pltpu.VMEM((1, width), jnp.int32),
            pltpu.VMEM(particle_velocity.shape, F32),
        ),
        in_specs=[hbm(), hbm(), smem(), hbm(), hbm(), hbm()],
        out_specs=(vmem(),) * 4,
        scratch_shapes=[
            pltpu.VMEM((1, requests), jnp.int32),
            pltpu.VMEM((1, requests), jnp.int32),
            pltpu.VMEM(particle_velocity.shape, F32),
            pltpu.VMEM((devices, pitch, 3 * span), BF16),
            pltpu.VMEM((devices, 1, 128), jnp.int32),
            pltpu.VMEM((1, slots), jnp.int32),
            pltpu.VMEM((3, lines, span), F32),
            pltpu.VMEM(interp_weight.shape, BF16),
            pltpu.VMEM((blocks // 2, cells, 2 * particles), BF16),
            pltpu.VMEM((devices, 128), jnp.int32),
            pltpu.VMEM((devices, 1, 128), jnp.int32),
            pltpu.SMEM((devices, 1, 128), jnp.int32),
            pltpu.VMEM((requests, 1), jnp.int32),
            pltpu.VMEM((1, requests), jnp.int32),
            pltpu.VMEM((3, pitch, span), F32),
            pltpu.VMEM((devices, pitch, 3 * span), BF16),
            pltpu.VMEM((devices, pitch, 3 * span), BF16),
            pltpu.VMEM((slots, 3 * span), F32),
            pltpu.VMEM((3, blocks, cells), F32),
            pltpu.VMEM((requests, 3 * span), F32),
            pltpu.VMEM((devices, pitch, 3 * span), BF16),
            pltpu.VMEM((3, 1, lines), F32),
            pltpu.VMEM((3, 1, lines), F32),
            pltpu.VMEM((9, wall, span), F32),
            pltpu.VMEM((9, wall, span), F32),
            pltpu.VMEM((3, 1, lines), F32),
            pltpu.VMEM((3, 1, lines), F32),
            pltpu.VMEM((9, wall, span), F32),
            pltpu.VMEM((9, wall, span), F32),
            dma((3,)),
            dma,
            dma,
            dma,
            dma((devices,)),
            dma((devices,)),
            dma((devices,)),
            dma((devices,)),
            dma((devices,)),
            dma((devices,)),
            dma((4,)),
            dma((4,)),
        ],
        compiler_params=pltpu.CompilerParams(
            vmem_limit_bytes=VMEM_LIMIT, collective_id=0, has_side_effects=True
        ),
        cost_estimate=cost(5e8, field_bytes + interp_weight.size * 2),
        name="step",
    )(
        in_hbm(tile_owner.reshape(1, requests)),
        in_hbm(tile_index.reshape(1, requests)),
        block_count,
        in_hbm(particle_velocity),
        in_hbm(velocity_field.reshape(3, lines, span)),
        in_hbm(interp_weight),
    )

    result, moved = pl.pallas_call(
        add_kernel,
        out_shape=(shape((3, lines, span), F32), shape(particle_velocity.shape, F32)),
        in_specs=[vmem()] * 4,
        out_specs=(hbm(), vmem()),
        scratch_shapes=[pltpu.VMEM((3, lines, span), F32), dma((PIECES if lines % (8 * PIECES) == 0 else 1,))],
        compiler_params=params(),
        cost_estimate=cost(2.0 * lines * width * 3 * span, field_bytes * 2),
        name="feedback",
    )(fluid, late, late_index, moved)
    return (result.reshape(velocity_field.shape), moved)


def solution(mesh):
    placed = (
        P(None, "gx", None, "gz"),
        P(("gx", "gz"), None, None),
        P(None, ("gx", "gz"), None),
        P(("gx", "gz"), None),
        P(("gx", "gz")),
        P(("gx", "gz")),
    )
    return jax.shard_map(
        shards,
        mesh=mesh,
        in_specs=placed,
        out_specs=(P(None, "gx", None, "gz"), P(None, ("gx", "gz"), None)),
        check_vma=False,
    )
```

```python
import functools
import math

import jax
import jax.numpy as jnp
from jax import lax
from jax.experimental import pallas as pl
from jax.experimental.pallas import tpu as pltpu
from jax.sharding import PartitionSpec as P

ROOT = (math.sqrt(5.0) / 3.0 - 1.0) * 1.5
GREEN_GAIN = 3.0 / math.sqrt(5.0)
GAMMA = (25.0 / 36.0) * GREEN_GAIN * (1.0 - ROOT * ROOT)
EPS = (1.0 / 12.0) / GAMMA
VISCOSITY = 0.2
RELAX_TIME = 1.0
TIME_STEP = 0.5
LOADING = 0.5
WINDOW = 48
EARLY = 1
CURVE = 2048
CURVE_EARLY = 2
SPREAD = 2048
PIECES = 6
F32 = jnp.float32
BF16 = jnp.bfloat16
VMEM_LIMIT = 40 * 1024 * 1024


def iota(shape, dim):
    return lax.broadcasted_iota(jnp.int32, shape, dim)


def dot(a, b, ca, cb):
    return lax.dot_general(a, b, (((ca,), (cb,)), ((), ())), preferred_element_type=F32)


def end_lanes(span):
    corner = (8, span)
    first = (iota(corner, 0) == 0) & (iota(corner, 1) == 0)
    second = (iota(corner, 0) == 1) & (iota(corner, 1) == span - 1)
    return jnp.where(first | second, 1.0, 0.0)


def halo_lanes(span):
    shape = (8, 3 * span)
    row, lane = iota(shape, 0), iota(shape, 1)
    first = (row == lane // span) & (lane % span == 0)
    last = (row == lane // span + 3) & (lane % span == span - 1)
    return jnp.where(first | last, 1.0, 0.0).astype(BF16)


def second_difference(span):
    shape = (2 * span, span)
    row, lane = iota(shape, 0) % span, iota(shape, 1)
    beside = (row == lane + 1) | (row + 1 == lane)
    return jnp.where(row == lane, -2.0, jnp.where(beside, 1.0, 0.0)).astype(BF16)


def request_slots(kt, pitch, gx, gz, x, z, owner_row, index_row):
    count, devices = owner_row.shape[1], gx * gz
    blocks = count // kt
    r = iota((count, 1), 0)
    cols = iota((count, count), 1)
    pick = cols == kt * (r % blocks) + r // blocks
    owner = jnp.sum(jnp.where(pick, owner_row, 0), 1, keepdims=True)
    index = jnp.sum(jnp.where(pick, index_row, 0), 1, keepdims=True)
    away = (owner // gz + (gx - x)) % gx - gx // 2
    turn = jnp.where(away > 0, 2 * away, jnp.where(away < 0, -2 * away - 1, 0))
    order = (gx - 1 - turn) * gz + (owner % gz + (2 * gz - z - 1)) % gz
    onehot = (order == iota((count, devices), 1)).astype(F32)
    lower = (cols <= r).astype(F32).astype(BF16)
    turned = onehot.astype(BF16)
    seen = dot(lower, turned, 1, 0)
    position = jnp.sum(seen * onehot, 1, keepdims=True).astype(jnp.int32) - 1
    slot = order * pitch + position
    place = slot % 128 == iota((count, 128), 1)
    high = jnp.where(place, (index // 128).astype(F32), 0.0).astype(BF16)
    low = jnp.where(place, (index % 128).astype(F32), 0.0).astype(BF16)
    high_sum, low_sum = dot(turned, high, 0, 0), dot(turned, low, 0, 0)
    send = high_sum.astype(jnp.int32) * 128 + low_sum.astype(jnp.int32)
    return slot, send


def advance(fields, carry):
    state, before = carry[:6], carry[6:]
    parts = [EPS * f + s for f, s in zip(before, state)]
    sums = [parts[3 + c] + fields[0] * parts[c] for c in range(3)]
    moved = [f + ROOT * s for f, s in zip(fields, state)]
    return sums, tuple(moved) + tuple(fields)


def step_kernel(
    sizes, owner_hbm, index_hbm, live_ref, velocity_hbm, field_hbm, weight_hbm,
    fluid_ref, late_ref, late_index_ref, moved_ref,
    owner_ref, index_ref, velocity_ref, back_ref, got_ref, names_ref, field_ref, weight_ref, turned_ref, table_ref, send_ref, got_smem, slot_ref, slot_row_ref, rows_ref, tile_ref, reply_ref,
    staged_ref, own_ref, push_ref, outgoing_ref,
    my_low, my_high, my_left, my_right, low_ref, high_ref, left_ref, right_ref,
    input_sem, field_sem, weight_sem, smem_sem, send_sem, recv_sem, tile_send, tile_recv, back_send, back_recv, edge_send, edge_recv,
):
    gx, gz, kt, window = sizes
    devices = gx * gz
    wall, span = my_left.shape[1:]
    lines = field_ref.shape[1]
    slab = lines // wall
    pitch = tile_ref.shape[1]
    slots = devices * pitch
    x, z = lax.axis_index("gx"), lax.axis_index("gz")
    inputs = [
        pltpu.make_async_copy(src, dst, input_sem.at[k])
        for k, (src, dst) in enumerate(((owner_hbm, owner_ref), (index_hbm, index_ref), (velocity_hbm, velocity_ref)))
    ]
    inputs[0].start()
    inputs[1].start()
    fetch = pltpu.make_async_copy(field_hbm, field_ref, field_sem)
    fetch_weight = pltpu.make_async_copy(weight_hbm, weight_ref, weight_sem)

    barrier = pltpu.get_barrier_semaphore()

    def peer(p, way):
        j = gx - 1 - p // gz
        dx = gx // 2 + (1 - 2 * (j % 2)) * ((j + 1) // 2)
        dz = p % gz + 1
        return lax.rem(x + way * dx + 2 * gx, gx), lax.rem(z + way * dz + 2 * gz, gz)

    mine = gz - 1

    def each(body, start=0, stop=devices):
        def one(u, carry):
            t = u // gz
            t = (1 - t % 2) * (t // 2) + t % 2 * (gx - 1 - t // 2)
            body(t * gz + u % gz)
            return carry

        if start <= mine:
            lax.fori_loop(start, mine, one, 0)
            start = mine + 1
        lax.fori_loop(start, stop, one, 0)

    def greet(p):
        pl.semaphore_signal(barrier, inc=1, device_id=peer(p, 1), device_id_type=pl.DeviceIdType.MESH)

    each(greet)
    fetch.start()
    inputs[0].wait()
    inputs[1].wait()
    slot, send = request_slots(kt, pitch, gx, gz, x, z, owner_ref[...], index_ref[...])
    slot_ref[...] = slot
    table_ref[...] = send
    for d in range(devices):
        send_ref[d] = table_ref[d : d + 1, :]
    pl.semaphore_wait(barrier, devices - 1)

    def exchange(src, dst, sent, got, way):
        def at(p):
            return pltpu.make_async_remote_copy(
                src_ref=src.at[p],
                dst_ref=dst.at[p],
                send_sem=sent.at[p],
                recv_sem=got.at[p],
                device_id=peer(p, way),
                device_id_type=pl.DeviceIdType.MESH,
            )

        return at

    parcel = exchange(send_ref, got_ref, send_sem, recv_sem, 1)
    tiles = exchange(tile_ref, reply_ref, tile_send, tile_recv, -1)
    pushes = exchange(outgoing_ref, back_ref, back_send, back_recv, 1)

    each(lambda n: parcel(n).start())
    got_ref[mine] = send_ref[mine]
    fetch.wait()
    fetch_weight.start()
    inputs[2].start()

    def edge(k, src, dst, peer):
        return pltpu.make_async_remote_copy(
            src_ref=src,
            dst_ref=dst,
            send_sem=edge_send.at[k],
            recv_sem=edge_recv.at[k],
            device_id=peer,
            device_id_type=pl.DeviceIdType.MESH,
        )

    edges = [
        edge(0, my_right, left_ref, (lax.rem(x + 1, gx), z)),
        edge(1, my_left, right_ref, (lax.rem(x + gx - 1, gx), z)),
        edge(2, my_high, low_ref, (x, lax.rem(z + 1, gz))),
        edge(3, my_low, high_ref, (x, lax.rem(z + gz - 1, gz))),
    ]

    def line(i):
        return pl.ds(pl.multiple_of(i * wall, wall), wall)

    def load(i):
        u = [field_ref[c, line(i), :] for c in range(3)]
        return u + [u[0] * u[c] for c in range(3)]

    zero = jnp.zeros((wall, span), F32)

    def moments(order):
        def one(i, state):
            return tuple(f + ROOT * s for f, s in zip(load(order(i)), state))

        return lax.fori_loop(0, window, one, (zero,) * 6, unroll=4)

    for k, value in enumerate(moments(lambda i: slab - window + i)):
        my_right[k] = value
    for c in range(3):
        my_right[6 + c] = field_ref[c, lines - wall :, :]
    edges[0].start()
    for k, value in enumerate(moments(lambda i: window - 1 - i)):
        my_left[k] = value
    for c in range(3):
        my_left[6 + c] = field_ref[c, :wall, :]
    edges[1].start()

    def up(i, carry):
        sums, carry = advance(load(i), carry)
        for c in range(3):
            fluid_ref[c, line(i), :] = 0.5 * GAMMA * sums[c]
        return carry

    ends = end_lanes(span).astype(BF16)
    span_rows = window
    for c in range(3):
        for n in range(slab // span_rows):
            part = slice(n * span_rows * wall, (n + 1) * span_rows * wall)
            lanes = dot(ends, field_ref[c, part].astype(BF16), 1, 1)
            my_low[c, :, part] = lanes[0:1]
            my_high[c, :, part] = lanes[1:2]
    edges[2].start()
    edges[3].start()
    early = slab * EARLY // 8
    carry = lax.fori_loop(0, early, up, (zero,) * 12, unroll=4)

    each(lambda n: parcel(n).wait())
    copy = pltpu.make_async_copy(got_ref, got_smem, smem_sem)
    copy.start()
    copy.wait()

    def collect(p):
        for k in range(pitch):
            row = jnp.minimum(jnp.maximum(got_smem[p, 0, lax.rem(p * pitch + k, 128)], 0), lines - 1)
            for c in range(3):
                rows_ref[c, k : k + 1, :] = field_ref[c, pl.ds(row, 1), :]
        for c in range(3):
            tile_ref[p, :, c * span : (c + 1) * span] = rows_ref[c].astype(BF16)

    def gather(p):
        collect(p)
        tiles(p).start()

    each(gather)
    collect(mine)
    reply_ref[mine] = tile_ref[mine]

    lax.fori_loop(early, slab, up, carry, unroll=4)

    particles, cells = weight_ref.shape[1:]
    fetch_weight.wait()

    def turn(n, carry):
        for b in range(2):
            turned_ref[n, :, b * particles : (b + 1) * particles] = jnp.transpose(weight_ref[2 * n + b])
        return carry

    lax.fori_loop(0, turned_ref.shape[0], turn, 0)
    edges[2].wait()
    edges[3].wait()
    long = CURVE if lines % CURVE == 0 else lines
    pick, curl = halo_lanes(span), second_difference(span)

    def curve(n, carry):
        at = pl.ds(pl.multiple_of(n * long, long), long)
        row = iota((8, long), 0)
        halo = jnp.zeros((8, long), F32)
        for c in range(3):
            halo = jnp.where(row == c, low_ref[c, :, at], jnp.where(row == c + 3, high_ref[c, :, at], halo))
        halo = dot(halo.astype(BF16), pick, 0, 0)
        for c in range(3):
            u = field_ref[c, at, :]
            head = u.astype(BF16)
            rest = (u - head.astype(F32)).astype(BF16)
            inside = dot(jnp.concatenate([head, rest], 1), curl, 1, 0)
            total = inside + halo[:, c * span : (c + 1) * span]
            fluid_ref[c, at, :] = fluid_ref[c, at, :] + VISCOSITY * total
        return carry

    half_way = lines // long * CURVE_EARLY // 4
    lax.fori_loop(0, half_way, curve, 0)

    count = slot_ref.shape[0]
    same = iota((count, count), 0) == iota((count, count), 1)
    slot_row_ref[...] = jnp.sum(jnp.where(same, slot_ref[...], 0), 0, keepdims=True)

    def stage(src, p):
        staged_ref[pl.ds(pl.multiple_of(p * pitch, pitch), pitch), :] = src[p].astype(F32)

    stage(reply_ref, mine)

    def receive(p):
        tiles(p).wait()
        stage(reply_ref, p)

    each(receive)

    blocks = count // kt
    chosen = jnp.where(slot_ref[...] == iota((count, slots), 1), 1.0, 0.0).astype(BF16)
    own = dot(chosen, staged_ref[...].astype(BF16), 1, 0)
    for j in range(kt):
        for c in range(3):
            own_ref[c, :, j * span : (j + 1) * span] = own[j * blocks : (j + 1) * blocks, c * span : (c + 1) * span]
    inputs[2].wait()
    group = 16 if blocks % 16 == 0 else 8
    live_blocks = live_ref[0]

    def particle(step, carry):
        base = pl.multiple_of(step * group, group)
        tile = jnp.concatenate([own_ref[c, pl.ds(base, group), :] for c in range(3)], 0).astype(BF16)
        row = iota((3 * group, particles), 0) % group
        sampled = jnp.zeros((3 * group, particles), F32)
        for b in range(0, group, 2):
            both = dot(tile, turned_ref[base // 2 + b // 2], 1, 0)
            sampled = jnp.where(row == b, both[:, :particles], sampled)
            sampled = jnp.where(row == b + 1, both[:, particles:], sampled)
        velocity = jnp.concatenate([velocity_ref[c, pl.ds(base, group), :] for c in range(3)], 0)
        live = jnp.where(row + base < live_blocks, 1.0, 0.0)
        drag = live * (sampled - velocity) * (1.0 / RELAX_TIME)
        moved = velocity + TIME_STEP * drag
        for c in range(3):
            moved_ref[c, pl.ds(base, group), :] = moved[c * group : (c + 1) * group]
        half = drag.astype(BF16)
        row = iota((3 * group, cells), 0) % group
        push = jnp.zeros((3 * group, cells), F32)
        for b in range(group):
            push = jnp.where(row == b, dot(half, weight_ref[base + b], 1, 0), push)
        push = -LOADING * push
        for j in range(kt):
            for c in range(3):
                push_ref[pl.ds(j * blocks + base, group), c * span : (c + 1) * span] = push[
                    c * group : (c + 1) * group, j * span : (j + 1) * span
                ]
        return carry

    lax.fori_loop(0, blocks // group, particle, 0, unroll=True)

    pushed = push_ref[...].astype(BF16)
    lot = 8
    chunks = devices // lot
    for q in sorted(range(chunks), key=lambda q: min(q, chunks - 1 - q)):
        named = jnp.where(iota((lot * pitch, count), 0) + q * lot * pitch == slot_row_ref[...], 1.0, 0.0).astype(BF16)
        placed = dot(named, pushed, 1, 0)
        for p in range(lot):
            outgoing_ref[q * lot + p] = placed[p * pitch : (p + 1) * pitch].astype(BF16)
        if q >= chunks // 2:
            ready = chunks - q
            each(lambda p: pushes(p).start(), 2 * lot * (ready - 1), 2 * lot * ready)
    back_ref[mine] = outgoing_ref[mine]

    def down(n, carry):
        i = slab - 1 - n
        sums, carry = advance(load(i), carry)
        for c in range(3):
            fluid_ref[c, line(i), :] = fluid_ref[c, line(i), :] - 0.5 * GAMMA * sums[c]
        return carry

    lax.fori_loop(0, slab, down, (zero,) * 12, unroll=4)

    def border(ref):
        u = [ref[6 + c] for c in range(3)]
        return [ref[k] for k in range(6)], u + [u[0] * u[c] for c in range(3)]

    def spread(ref, gain, order):
        state, before = border(ref)

        def add(i, parts):
            u0 = field_ref[0, line(i), :]
            for c in range(3):
                fluid_ref[c, line(i), :] = fluid_ref[c, line(i), :] + gain * (parts[3 + c] + u0 * parts[c])

        add(order(0), [EPS * f + s for f, s in zip(before, state)])

        def one(n, state):
            add(order(n), state)
            return tuple(ROOT * s for s in state)

        lax.fori_loop(1, window, one, tuple(ROOT * s for s in state), unroll=2)

    edges[0].wait()
    spread(left_ref, 0.5 * GAMMA, lambda n: n)
    edges[1].wait()
    spread(right_ref, -0.5 * GAMMA, lambda n: slab - 1 - n)

    lax.fori_loop(half_way, lines // long, curve, 0)
    for g in range(slots // 128):
        row = jnp.zeros((1, 128), jnp.int32)
        for p in range(g * 128 // pitch, min(devices, (g * 128 + 127) // pitch + 1)):
            flat = iota((1, 128), 1) + (g * 128 - p * pitch)
            row = jnp.where((flat >= 0) & (flat < pitch), got_ref[p], row)
        names_ref[:, g * 128 : (g + 1) * 128] = row

    def take(p, carry):
        pushes(p).wait()
        stage(back_ref, p)
        return carry

    soon = slots - late_ref.shape[0]
    first = -(-soon // pitch)
    stage(back_ref, mine)
    lax.fori_loop(0, mine, take, 0)
    lax.fori_loop(mine + 1, first, take, 0)
    size = SPREAD if lines % SPREAD == 0 else lines
    batch = staged_ref[:soon, :].astype(BF16)

    def returned(n, carry):
        at = pl.ds(pl.multiple_of(n * size, size), size)
        named = jnp.where(iota((size, soon), 0) + n * size == names_ref[:, :soon], 1.0, 0.0).astype(BF16)
        total = dot(named, batch, 1, 0)
        for c in range(3):
            fluid_ref[c, at, :] = fluid_ref[c, at, :] + total[:, c * span : (c + 1) * span]
        return carry

    lax.fori_loop(0, lines // size, returned, 0)
    lax.fori_loop(first, devices, take, 0)
    late_ref[...] = staged_ref[soon:, :].astype(BF16)
    late_index_ref[...] = names_ref[:, soon:]


def add_kernel(fluid_ref, late_ref, late_index_ref, moved_ref, out_hbm, moved_out, out_ref, out_sem):
    lines, span = fluid_ref.shape[1:]
    size = lines // out_sem.shape[0]
    width = late_ref.shape[0]

    def leave(n):
        at = pl.ds(pl.multiple_of(n * size, size), size)
        return pltpu.make_async_copy(out_ref.at[:, at, :], out_hbm.at[:, at, :], out_sem.at[n])

    def one(n, carry):
        named = jnp.where(iota((size, width), 0) + n * size == late_index_ref[...], 1.0, 0.0).astype(BF16)
        total = dot(named, late_ref[...], 1, 0)
        at = pl.ds(pl.multiple_of(n * size, size), size)
        for c in range(3):
            out_ref[c, at, :] = fluid_ref[c, at, :] + total[:, c * span : (c + 1) * span]
        leave(n).start()
        return carry

    lax.fori_loop(0, lines // size, one, 0)
    moved_out[...] = moved_ref[...]

    def finish(n, carry):
        leave(n).wait()
        return carry

    lax.fori_loop(0, lines // size, finish, 0)


def vmem():
    return pl.BlockSpec(memory_space=pltpu.VMEM)


def smem():
    return pl.BlockSpec(memory_space=pltpu.SMEM)


def hbm():
    return pl.BlockSpec(memory_space=pltpu.HBM)


def params():
    return pltpu.CompilerParams(vmem_limit_bytes=VMEM_LIMIT)


def cost(flops, nbytes):
    return pl.CostEstimate(flops=int(flops), bytes_accessed=int(nbytes), transcendentals=0)


def in_hbm(array):
    return pltpu.with_memory_space_constraint(array, pltpu.HBM)


def shards(velocity_field, interp_weight, particle_velocity, tile_owner, tile_index, block_count):
    _, slab, wall, span = velocity_field.shape
    shape = jax.ShapeDtypeStruct
    gx, gz = lax.axis_size("gx"), lax.axis_size("gz")
    devices = gx * gz
    requests = tile_index.shape[0]
    blocks, particles, cells = interp_weight.shape
    kt = requests // blocks
    pitch = -(-max(2, 3 * requests // devices) // 8) * 8
    slots = devices * pitch
    field_bytes = velocity_field.size * 4

    window = WINDOW if slab % WINDOW == 0 else slab
    lines = slab * wall
    dma = pltpu.SemaphoreType.DMA
    width = slots - 256
    fluid, late, late_index, moved = pl.pallas_call(
        functools.partial(step_kernel, (gx, gz, kt, window)),
        out_shape=(
            pltpu.VMEM((3, lines, span), F32),
            pltpu.VMEM((width, 3 * span), BF16),
            pltpu.VMEM((1, width), jnp.int32),
            pltpu.VMEM(particle_velocity.shape, F32),
        ),
        in_specs=[hbm(), hbm(), smem(), hbm(), hbm(), hbm()],
        out_specs=(vmem(),) * 4,
        scratch_shapes=[
            pltpu.VMEM((1, requests), jnp.int32),
            pltpu.VMEM((1, requests), jnp.int32),
            pltpu.VMEM(particle_velocity.shape, F32),
            pltpu.VMEM((devices, pitch, 3 * span), BF16),
            pltpu.VMEM((devices, 1, 128), jnp.int32),
            pltpu.VMEM((1, slots), jnp.int32),
            pltpu.VMEM((3, lines, span), F32),
            pltpu.VMEM(interp_weight.shape, BF16),
            pltpu.VMEM((blocks // 2, cells, 2 * particles), BF16),
            pltpu.VMEM((devices, 128), jnp.int32),
            pltpu.VMEM((devices, 1, 128), jnp.int32),
            pltpu.SMEM((devices, 1, 128), jnp.int32),
            pltpu.VMEM((requests, 1), jnp.int32),
            pltpu.VMEM((1, requests), jnp.int32),
            pltpu.VMEM((3, pitch, span), F32),
            pltpu.VMEM((devices, pitch, 3 * span), BF16),
            pltpu.VMEM((devices, pitch, 3 * span), BF16),
            pltpu.VMEM((slots, 3 * span), F32),
            pltpu.VMEM((3, blocks, cells), F32),
            pltpu.VMEM((requests, 3 * span), F32),
            pltpu.VMEM((devices, pitch, 3 * span), BF16),
            pltpu.VMEM((3, 1, lines), F32),
            pltpu.VMEM((3, 1, lines), F32),
            pltpu.VMEM((9, wall, span), F32),
            pltpu.VMEM((9, wall, span), F32),
            pltpu.VMEM((3, 1, lines), F32),
            pltpu.VMEM((3, 1, lines), F32),
            pltpu.VMEM((9, wall, span), F32),
            pltpu.VMEM((9, wall, span), F32),
            dma((3,)),
            dma,
            dma,
            dma,
            dma((devices,)),
            dma((devices,)),
            dma((devices,)),
            dma((devices,)),
            dma((devices,)),
            dma((devices,)),
            dma((4,)),
            dma((4,)),
        ],
        compiler_params=pltpu.CompilerParams(
            vmem_limit_bytes=VMEM_LIMIT, collective_id=0, has_side_effects=True
        ),
        cost_estimate=cost(5e8, field_bytes + interp_weight.size * 2),
        name="step",
    )(
        in_hbm(tile_owner.reshape(1, requests)),
        in_hbm(tile_index.reshape(1, requests)),
        block_count,
        in_hbm(particle_velocity),
        in_hbm(velocity_field.reshape(3, lines, span)),
        in_hbm(interp_weight),
    )

    result, moved = pl.pallas_call(
        add_kernel,
        out_shape=(shape((3, lines, span), F32), shape(particle_velocity.shape, F32)),
        in_specs=[vmem()] * 4,
        out_specs=(hbm(), vmem()),
        scratch_shapes=[pltpu.VMEM((3, lines, span), F32), dma((PIECES if lines % (8 * PIECES) == 0 else 1,))],
        compiler_params=params(),
        cost_estimate=cost(2.0 * lines * width * 3 * span, field_bytes * 2),
        name="feedback",
    )(fluid, late, late_index, moved)
    return (result.reshape(velocity_field.shape), moved)


def solution(mesh):
    placed = (
        P(None, "gx", None, "gz"),
        P(("gx", "gz"), None, None),
        P(None, ("gx", "gz"), None),
        P(("gx", "gz"), None),
        P(("gx", "gz")),
        P(("gx", "gz")),
    )
    return jax.shard_map(
        shards,
        mesh=mesh,
        in_specs=placed,
        out_specs=(P(None, "gx", None, "gz"), P(None, ("gx", "gz"), None)),
        check_vma=False,
    )
```
